128 devices in a mesh: gx: 16 (over z, x), gy: 8 (over y, core).
Axes of the slice: x: 4, y: 4, z: 4, core: 2. Of those that a mesh axis runs over, the one named last changes fastest.
Arguments:
- innovations: bfloat16 [128, 64, 512], P(('gx', 'gy')), may hold values from -18 to 18
- station_columns: int32 [128, 512], P(('gx', 'gy')), may hold values from 0 to 4095
- profile_counts: int32 [128, 128], P(('gx', 'gy')), may hold values from 0 to 4, as said below
- land_mask: int32 [128, 4096], P('gy', 'gx'), may hold values 0 or 1
- vertical_coef: float32 [32, 128, 4096], P(None, 'gy', 'gx'), may hold values from 0.3 to 30
- inverse_x: bfloat16 [2, 4096, 4096], P(None, None, 'gx')
- inverse_y: bfloat16 [2, 128, 128], replicated
Outputs:
- increment: bfloat16 [64, 128, 4096], P(None, 'gy', 'gx')
- equivalents: bfloat16 [128, 64, 512], P(('gx', 'gy'))
The draws below stay inside these ranges and needn't reach their ends.
Inputs may be any that keep to these rules, and one draw needn't show every extreme that they name: `profile_counts`: every draw has one owner device that receives 4 live profiles from every device.
All inputs are finite; a program needn't handle non-finite values. No bound on the sum of `land_mask` on one device may be relied on, other than what follows from the above.
Results may differ from the reference program's by a relative error of at most 0.0061.
Values may be sent and summed in bfloat16 or wider, within the bound.
No kernel may reach another device: no remote copies, remote signals or barrier semaphores. Data moves between devices by JAX's collectives and lax.ppermute only.
A program may use at most 64 MiB of HBM per device.

```python
import math
import jax
import jax.numpy as jnp

LEV = 32
CAP = 4
NX = 4096
CY = 16
CX = 256
LAYERS = 64
NY = 128
N_GX = 16
N_GY = 8
DEVICES = 128


def draw_profile_counts(key, part):
    key_hot = jax.random.fold_in(key, 11)
    key_cap = jax.random.fold_in(key, 12)
    key_base = jax.random.fold_in(key, 13)
    hot_owner = jax.random.randint(key_hot, (), 0, DEVICES)
    owner_cap = jax.random.randint(key_cap, (DEVICES,), 2, CAP + 1)
    base_draw = jax.random.randint(key_base, (DEVICES, DEVICES), 0, CAP + 1)
    limited = jnp.minimum(base_draw, owner_cap[None, :])
    owner_ids = jnp.arange(DEVICES, dtype=jnp.int32)[None, :]
    return jnp.where(owner_ids == hot_owner, CAP, limited).astype(jnp.int32)


def draw_inverse_x(key, part):
    key_scale = jax.random.fold_in(key, 21)
    key_factor = jax.random.fold_in(key, 22)
    positions = jnp.arange(NX, dtype=jnp.int32)
    distance = jnp.abs(positions[:, None] - positions[None, :])
    distance = jnp.minimum(distance, NX - distance).astype(jnp.float32)
    length_scale = jnp.exp(jax.random.uniform(key_scale, (2, 1, NX), jnp.float32, math.log(NX / 8.0), math.log(NX * 1.0)))
    factor = jax.random.uniform(key_factor, (2, NX, NX), jnp.float32, 0.5, 1.5)
    return (factor * jnp.exp(-distance[None, :, :] / length_scale) / jnp.sqrt(length_scale)).astype(jnp.bfloat16)


def draw_inverse_y(key, part):
    key_scale = jax.random.fold_in(key, 31)
    key_factor = jax.random.fold_in(key, 32)
    positions = jnp.arange(NY, dtype=jnp.int32)
    distance = jnp.abs(positions[:, None] - positions[None, :]).astype(jnp.float32)
    length_scale = jnp.exp(jax.random.uniform(key_scale, (2, 1, NY), jnp.float32, math.log(NY / 4.0), math.log(NY * 2.0)))
    factor = jax.random.uniform(key_factor, (2, NY, NY), jnp.float32, 0.5, 1.5)
    return (factor * jnp.exp(-distance[None, :, :] / length_scale) / jnp.sqrt(length_scale)).astype(jnp.bfloat16)


def place_ends(entries, own_key, least, largest):
    index_at = [jax.random.randint(jax.random.fold_in(own_key, axis), (), 0, length) for axis, length in enumerate(entries.shape)]
    main_axis = entries.shape.index(max(entries.shape))
    neighbour = index_at[:main_axis] + [(index_at[main_axis] + 1) % entries.shape[main_axis]] + index_at[main_axis + 1:]
    return entries.at[tuple(index_at)].set(least).at[tuple(neighbour)].set(largest)


def steps_of(own_key, extent, split, smallest, high):
    def one(dim, blocks):
        heights = jax.random.uniform(jax.random.fold_in(jax.random.fold_in(own_key, 6), dim), (blocks,), jnp.float32, smallest / len(split), high / len(split))
        return jnp.repeat(jnp.exp(heights), extent[dim] // blocks).reshape((-1,) + (1,) * (len(extent) - dim - 1))

    gain = one(*split[0])
    for cut in split[1:]:
        gain = gain * one(*cut)
    return gain


def normal_values(stream_key, dims, scale, reach, shards=(), held_as=jnp.bfloat16):
    values = jax.random.normal(stream_key, dims, jnp.float32) * scale
    if len(shards) > 0:
        values = steps_of(stream_key, dims, shards, -0.22, 0.18) * values
    return jnp.clip(values, min=-reach, max=reach).astype(held_as)


def setup_inputs(seed: int = 0) -> dict:
    seeds = jax.random.split(jax.random.key(seed), 8)
    return {
        "innovations": normal_values(seeds[0], (DEVICES, LAYERS, DEVICES * CAP), 3.0, 18.0, ((0, 128),)),
        "station_columns": place_ends(jax.random.randint(seeds[1], (DEVICES, DEVICES * CAP), 0, CY * CX), jax.random.fold_in(seeds[1], 1), 0, (CY * CX) - 1).astype(jnp.int32),
        "profile_counts": draw_profile_counts(jax.random.fold_in(seeds[7], 71), 0),
        "land_mask": place_ends((jax.random.randint(seeds[3], (NY, NX), 0, 4) < 3).astype(jnp.int32), jax.random.fold_in(seeds[3], 1), 0, 1),
        "vertical_coef": jnp.clip(jnp.exp(math.log(30.0) - 4.6051701 * jax.random.uniform(seeds[4], (LEV, NY, NX), jnp.float32) ** steps_of(seeds[4], (LEV, NY, NX), ((1, 8), (2, 16)), -0.2, 0.2)), 0.3, 30.0),
        "inverse_x": draw_inverse_x(jax.random.fold_in(seeds[7], 71), 0),
        "inverse_y": draw_inverse_y(jax.random.fold_in(seeds[7], 71), 0),
    }


def vertical_solve(rhs_field, coupling):
    levels = coupling.shape[0]
    zero_row = jnp.zeros_like(coupling[0])
    ratios = []
    partial_sol = []
    for level in range(levels):
        upper_coef = coupling[level + 1] if level + 1 < levels else zero_row
        diagonal = 1.0 + coupling[level] + upper_coef
        if level == 0:
            denominator = diagonal
            carried = rhs_field[:, 0]
        else:
            denominator = diagonal + coupling[level] * ratios[-1]
            carried = rhs_field[:, level] + coupling[level] * partial_sol[-1]
        ratios.append(-upper_coef / denominator)
        partial_sol.append(carried / denominator)
    solution = [partial_sol[-1]]
    for level in range(levels - 2, -1, -1):
        solution.append(partial_sol[level] - ratios[level] * solution[-1])
    return jnp.stack(solution[::-1], axis=1)


def reference(innovations, station_columns, profile_counts, land_mask, vertical_coef, inverse_x, inverse_y):
    devices_all = N_GX * N_GY
    layers = 2 * LEV
    slot_index = jnp.arange(CAP, dtype=jnp.int32)
    live = slot_index[None, None, :] < profile_counts[:, :, None]
    values = innovations.reshape(devices_all, layers, devices_all, CAP).astype(jnp.float32)
    values = jnp.where(live[:, None, :, :], values, jnp.zeros((), jnp.float32))
    owners = jnp.arange(devices_all, dtype=jnp.int32)
    owners_x = owners // N_GY
    owners_y = owners % N_GY
    local_cols = station_columns.reshape(devices_all, devices_all, CAP)
    global_index = (owners_y[:, None, None] * CY + local_cols // CX) * NX + owners_x[:, None, None] * CX + local_cols % CX
    flat_index = global_index.reshape(-1).astype(jnp.int32)
    ordered = jnp.transpose(values, (1, 2, 0, 3)).reshape(layers, devices_all * devices_all * CAP)
    gridded = jnp.zeros((layers, NY * NX), jnp.float32).at[:, flat_index].add(ordered)
    mask_field = land_mask.astype(jnp.float32).reshape(NY * NX)
    start_field = (gridded * mask_field).astype(jnp.bfloat16).reshape(2, LEV, NY, NX)
    results = []
    for tracer in range(2):
        along_x = jnp.dot(start_field[tracer].reshape(LEV * NY, NX), inverse_x[tracer], preferred_element_type=jnp.float32)
        along_x = along_x.astype(jnp.bfloat16).reshape(LEV, NY, NX)
        along_y = jnp.einsum("jm,kjc->kmc", inverse_y[tracer].astype(jnp.float32), along_x.astype(jnp.float32))
        results.append(along_y.astype(jnp.bfloat16))
    column_field = jnp.stack(results).astype(jnp.float32).reshape(2, LEV, NY * NX)
    solved = vertical_solve(column_field, vertical_coef.reshape(LEV, NY * NX))
    increment = (solved * mask_field[None, None, :]).astype(jnp.bfloat16).reshape(layers, NY, NX)
    picked = increment.reshape(layers, NY * NX)[:, flat_index].reshape(layers, devices_all, devices_all, CAP)
    picked = jnp.transpose(picked, (2, 0, 1, 3))
    equivalents = jnp.where(live[:, None, :, :], picked, jnp.zeros((), jnp.bfloat16))
    return increment, equivalents.reshape(devices_all, layers, devices_all * CAP)
```

```python
import functools
import jax
import jax.numpy as jnp
from jax import lax
from jax.experimental import pallas as pl
from jax.experimental.pallas import tpu as pltpu
from jax.sharding import PartitionSpec as P

LEV = 32
CAP = 4
CY = 16
CX = 256
LAYERS = 64
NY = 128
N_GX = 16
N_GY = 8
DEV = 128
SLOTS = DEV * CAP
SHARE = LAYERS // N_GY
ROWS = 40
BF = jnp.bfloat16
F32 = jnp.float32
I32 = jnp.int32


def iota(shape, dim):
    return lax.broadcasted_iota(I32, shape, dim)


def one_hot(cond):
    return jnp.where(cond, 1.0, 0.0).astype(BF)


def dot(a, b, dims=((1,), (0,))):
    return lax.dot_general(a, b, (dims, ((), ())), preferred_element_type=F32)


def send_kernel(inn_ref, col_ref, cnt_ref, mask_ref, out_ref):
    counts = jnp.broadcast_to(cnt_ref[...], (8, DEV)).astype(F32).astype(BF)
    spread = one_hot(iota((DEV, SLOTS), 1) // CAP == iota((DEV, SLOTS), 0))
    count_lane = dot(counts, spread)[0:1, :]
    slot_lane = (iota((1, SLOTS), 1) % CAP).astype(F32)
    live = slot_lane < count_lane
    values = jnp.where(live, inn_ref[0].astype(F32), 0.0).astype(BF)
    cells = col_ref[...]
    row = cells // CX
    col = cells % CX
    pick_col = one_hot(iota((CX, SLOTS), 0) == col)
    sea_rows = dot(mask_ref[...].astype(F32).astype(BF), pick_col)
    sea = jnp.sum(jnp.where(iota((CY, SLOTS), 0) == row, sea_rows, 0.0), axis=0, keepdims=True)
    row_code = jnp.where(sea > 0.5, row.astype(F32), 255.0)
    codes = jnp.where(
        iota((8, SLOTS), 0) == 0,
        jnp.broadcast_to(row_code, (8, SLOTS)),
        jnp.broadcast_to(col.astype(F32), (8, SLOTS)),
    ).astype(BF)
    source = iota((SLOTS, SLOTS), 0)
    target = iota((SLOTS, SLOTS), 1)
    permute = one_hot((source % CAP) * DEV + source // CAP == target)
    moved = dot(codes, permute)
    tile = jnp.concatenate(
        [moved[0:1, c * DEV : (c + 1) * DEV] for c in range(CAP)]
        + [moved[1:2, c * DEV : (c + 1) * DEV] for c in range(CAP)],
        axis=0,
    ).astype(BF)
    for b in range(N_GY):
        block = values[b * SHARE : (b + 1) * SHARE, :]
        message = jnp.concatenate(
            [block[:, q * DEV : (q + 1) * DEV] for q in range(CAP)] + [tile], axis=0
        )
        for a in range(N_GX):
            out_ref[a * N_GY + b] = message


def smooth_kernel(tracer_ref, got_ref, kx_ref, ky_ref, out_ref, wide_ref, turned_ref, dense_ref, acc_ref):
    step = pl.program_id(0)

    @pl.when(step == 0)
    def _():
        acc_ref[...] = jnp.zeros_like(acc_ref)

        def widen(s, carry):
            wide_ref[pl.ds(pl.multiple_of(s * 32, 32), 32), :] = got_ref[s, 0:32, :].astype(F32)
            return carry

        lax.fori_loop(0, DEV, widen, 0, unroll=8)
        for q in range(CAP):
            for l in range(SHARE):
                block = wide_ref[pl.ds(q * SHARE + l, DEV, stride=32), :]
                turned_ref[pl.ds(q * DEV * SHARE + l, DEV, stride=SHARE), :] = block.T

    col_iota = iota((CX, DEV), 0).astype(F32).astype(BF)
    half_iota = (iota((2 * SHARE, DEV), 0) // SHARE).astype(F32).astype(BF)
    zero = jnp.zeros((), BF)
    one = jnp.ones((), BF)
    for b in range(N_GY):
        owner = step * N_GY + b
        codes = got_ref[owner, 32:40, :].astype(F32)
        left = [[] for _ in range(N_GY)]
        right = []
        for c in range(CAP):
            base = pl.multiple_of(owner * (CAP * SHARE) + c * SHARE, SHARE)
            v = turned_ref[pl.ds(base, SHARE), :]
            twice = jnp.concatenate([v, v], axis=0).astype(BF)
            row = jnp.broadcast_to(codes[c : c + 1, :], (2 * SHARE, DEV)).astype(BF)
            pair = row - half_iota
            for k in range(CY // 2):
                left[k].append(jnp.where(pair == jnp.asarray(2 * k, BF), twice, zero))
            col = jnp.broadcast_to(codes[CAP + c : CAP + c + 1, :], (CX, DEV)).astype(BF)
            right.append(jnp.where(col == col_iota, one, zero))
        lhs = jnp.concatenate([jnp.concatenate(x, axis=1) for x in left], axis=0)
        rhs = jnp.concatenate(right, axis=1)
        dense = dot(lhs, rhs, ((1,), (1,)))
        dense_ref[b * 128 : (b + 1) * 128, :] = dense.astype(BF)
    gain = dot(dense_ref[...], kx_ref[0])
    for h in range(2):
        acc_ref[h * 1024 : (h + 1) * 1024, :] += gain[:, h * 128 : (h + 1) * 128]

    @pl.when(step == N_GX - 1)
    def _():
        for l in range(SHARE):
            along_x = jnp.concatenate(
                [acc_ref[pl.ds(h * 1024 + l, NY, stride=SHARE), :] for h in range(2)], axis=1
            ).astype(BF)
            along_y = dot(ky_ref[0], along_x, ((0,), (0,))).astype(BF)
            for b in range(N_GY):
                out_ref[b, l] = along_y[b * CY : (b + 1) * CY, :]


def solve_kernel(field_ref, coef_ref, mask_ref, col_ref, inc_ref, pick_ref, part_ref, ratio_ref):
    mask = mask_ref[...].astype(F32)
    prev0 = prev1 = ratio = None
    for k in range(LEV):
        here = coef_ref[k]
        below = coef_ref[k + 1] if k + 1 < LEV else jnp.zeros_like(here)
        f0 = field_ref[k].astype(F32)
        f1 = field_ref[LEV + k].astype(F32)
        diagonal = 1.0 + here + below
        if k == 0:
            inv = 1.0 / diagonal
            prev0 = f0 * inv
            prev1 = f1 * inv
        else:
            inv = 1.0 / (diagonal + here * ratio)
            prev0 = (f0 + here * prev0) * inv
            prev1 = (f1 + here * prev1) * inv
        ratio = -below * inv
        ratio_ref[k] = ratio
        part_ref[k] = prev0
        part_ref[LEV + k] = prev1
    x0 = x1 = None
    for k in range(LEV - 1, -1, -1):
        if k == LEV - 1:
            x0 = part_ref[k]
            x1 = part_ref[LEV + k]
        else:
            x0 = part_ref[k] - ratio_ref[k] * x0
            x1 = part_ref[LEV + k] - ratio_ref[k] * x1
        inc_ref[k] = (x0 * mask).astype(BF)
        inc_ref[LEV + k] = (x1 * mask).astype(BF)
    cells = col_ref[...]
    row = cells // CX
    col = cells % CX
    pick_col = one_hot(iota((CX, SLOTS), 0) == col)
    row_iota = iota((LAYERS * CY, SLOTS), 0) % CY
    found = dot(inc_ref[...].reshape(LAYERS * CY, CX), pick_col)
    chosen = jnp.where(row_iota == row, found, 0.0).astype(BF)
    total = one_hot(iota((LAYERS, LAYERS * CY), 1) // CY == iota((LAYERS, LAYERS * CY), 0))
    pick_ref[...] = dot(chosen, total, ((0,), (1,))).astype(BF)


def call(kernel, out_shape, n_in, name, scratch=()):
    return pl.pallas_call(
        kernel,
        out_shape=out_shape,
        in_specs=[pl.BlockSpec(memory_space=pltpu.VMEM)] * n_in,
        out_specs=jax.tree.map(lambda _: pl.BlockSpec(memory_space=pltpu.VMEM), out_shape),
        scratch_shapes=list(scratch),
        name=name,
    )


def body(innovations, station_columns, profile_counts, land_mask, vertical_coef, inverse_x, inverse_y):
    everyone = ("gx", "gy")
    message = call(send_kernel, jax.ShapeDtypeStruct((DEV, ROWS, DEV), BF), 4, "send")(
        innovations, station_columns, profile_counts, land_mask
    )
    got = lax.all_to_all(message, everyone, split_axis=0, concat_axis=0, tiled=True)
    tracer = (lax.axis_index("gy") * SHARE // LEV).reshape(1).astype(I32)
    product = pl.pallas_call(
        smooth_kernel,
        out_shape=jax.ShapeDtypeStruct((N_GY, SHARE, CY, CX), BF),
        grid_spec=pltpu.PrefetchScalarGridSpec(
            num_scalar_prefetch=1,
            grid=(N_GX,),
            in_specs=[
                pl.BlockSpec((DEV, ROWS, DEV), lambda i, t: (0, 0, 0), pipeline_mode=pl.Buffered(1)),
                pl.BlockSpec((1, CX, CX), lambda i, t: (t[0], i, 0)),
                pl.BlockSpec((1, NY, NY), lambda i, t: (t[0], 0, 0)),
            ],
            out_specs=pl.BlockSpec((N_GY, SHARE, CY, CX), lambda i, t: (0, 0, 0, 0)),
            scratch_shapes=[
                pltpu.VMEM((DEV * 32, DEV), F32),
                pltpu.VMEM((SLOTS * SHARE, DEV), F32),
                pltpu.VMEM((NY * SHARE, CX), BF),
                pltpu.VMEM((2 * NY * SHARE, 128), F32),
            ],
        ),
        compiler_params=pltpu.CompilerParams(dimension_semantics=("arbitrary",)),
        name="smooth",
    )(tracer, got, inverse_x, inverse_y)
    along_y = lax.all_to_all(product, "gy", split_axis=0, concat_axis=0, tiled=True)
    increment, picked = call(
        solve_kernel,
        (jax.ShapeDtypeStruct((LAYERS, CY, CX), BF), jax.ShapeDtypeStruct((SLOTS, LAYERS), BF)),
        4,
        "solve",
        [pltpu.VMEM((LAYERS, CY, CX), F32), pltpu.VMEM((LEV, CY, CX), F32)],
    )(along_y.reshape(LAYERS, CY, CX), vertical_coef, land_mask, station_columns)
    returned = lax.all_to_all(
        picked.reshape(DEV, 2, 128), everyone, split_axis=0, concat_axis=0, tiled=True
    )
    returned = returned.reshape(SLOTS, LAYERS).T.reshape(1, LAYERS, SLOTS)
    slot_index = lax.broadcasted_iota(I32, (DEV, CAP), 1)
    live = (slot_index < profile_counts[0][:, None]).reshape(SLOTS)
    equivalents = jnp.where(live[None, None, :], returned, jnp.zeros((), BF))
    return increment, equivalents


def solution(mesh):
    in_specs = (
        P(("gx", "gy"), None, None),
        P(("gx", "gy"), None),
        P(("gx", "gy"), None),
        P("gy", "gx"),
        P(None, "gy", "gx"),
        P(None, None, "gx"),
        P(),
    )
    out_specs = (P(None, "gy", "gx"), P(("gx", "gy"), None, None))
    return jax.shard_map(body, mesh=mesh, in_specs=in_specs, out_specs=out_specs, check_vma=False)
```

```python
import functools
import jax
import jax.numpy as jnp
from jax import lax
from jax.experimental import pallas as pl
from jax.experimental.pallas import tpu as pltpu
from jax.sharding import PartitionSpec as P

LEV = 32
CAP = 4
CY = 16
CX = 256
LAYERS = 64
NY = 128
N_GX = 16
N_GY = 8
DEV = 128
SLOTS = DEV * CAP
SHARE = LAYERS // N_GY
ROWS = 40
BF = jnp.bfloat16
F32 = jnp.float32
I32 = jnp.int32


def iota(shape, dim):
    return lax.broadcasted_iota(I32, shape, dim)


def one_hot(cond):
    return jnp.where(cond, 1.0, 0.0).astype(BF)


def dot(a, b, dims=((1,), (0,))):
    return lax.dot_general(a, b, (dims, ((), ())), preferred_element_type=F32)


def send_kernel(inn_ref, col_ref, cnt_ref, mask_ref, out_ref):
    counts = jnp.broadcast_to(cnt_ref[...], (8, DEV)).astype(F32).astype(BF)
    spread = one_hot(iota((DEV, SLOTS), 1) // CAP == iota((DEV, SLOTS), 0))
    count_lane = dot(counts, spread)[0:1, :]
    slot_lane = (iota((1, SLOTS), 1) % CAP).astype(F32)
    live = slot_lane < count_lane
    values = jnp.where(live, inn_ref[0].astype(F32), 0.0).astype(BF)
    cells = col_ref[...]
    row = cells // CX
    col = cells % CX
    pick_col = one_hot(iota((CX, SLOTS), 0) == col)
    sea_rows = dot(mask_ref[...].astype(F32).astype(BF), pick_col)
    sea = jnp.sum(jnp.where(iota((CY, SLOTS), 0) == row, sea_rows, 0.0), axis=0, keepdims=True)
    row_code = jnp.where(sea > 0.5, row.astype(F32), 255.0)
    codes = jnp.where(
        iota((8, SLOTS), 0) == 0,
        jnp.broadcast_to(row_code, (8, SLOTS)),
        jnp.broadcast_to(col.astype(F32), (8, SLOTS)),
    ).astype(BF)
    source = iota((SLOTS, SLOTS), 0)
    target = iota((SLOTS, SLOTS), 1)
    permute = one_hot((source % CAP) * DEV + source // CAP == target)
    moved = dot(codes, permute)
    tile = jnp.concatenate(
        [moved[0:1, c * DEV : (c + 1) * DEV] for c in range(CAP)]
        + [moved[1:2, c * DEV : (c + 1) * DEV] for c in range(CAP)],
        axis=0,
    ).astype(BF)
    for b in range(N_GY):
        block = values[b * SHARE : (b + 1) * SHARE, :]
        message = jnp.concatenate(
            [block[:, q * DEV : (q + 1) * DEV] for q in range(CAP)] + [tile], axis=0
        )
        for a in range(N_GX):
            out_ref[a * N_GY + b] = message


def smooth_kernel(
    tracer_ref, got_ref, kx_ref, ky_ref, *refs
):
    out_refs = refs[:N_GY]
    wide_ref, turned_ref, dense_ref, acc_ref, along_ref, kx_vmem, sem = refs[N_GY:]
    fetch = pltpu.make_async_copy(kx_ref.at[tracer_ref[0]], kx_vmem, sem)
    fetch.start()
    acc_ref[...] = jnp.zeros_like(acc_ref)

    def widen(s, carry):
        wide_ref[pl.ds(pl.multiple_of(s * 32, 32), 32), :] = got_ref[s, 0:32, :].astype(F32)
        return carry

    lax.fori_loop(0, DEV, widen, 0, unroll=8)
    for q in range(CAP):
        for l in range(SHARE):
            block = wide_ref[pl.ds(q * SHARE + l, DEV, stride=32), :]
            turned_ref[pl.ds(q * DEV * SHARE + l, DEV, stride=SHARE), :] = block.T
    fetch.wait()

    col_iota = iota((CX, DEV), 0).astype(F32).astype(BF)
    half_iota = (iota((2 * SHARE, DEV), 0) // SHARE).astype(F32).astype(BF)
    zero = jnp.zeros((), BF)
    one = jnp.ones((), BF)

    def column_block(step, carry):
        for b in range(N_GY):
            owner = step * N_GY + b
            codes = got_ref[owner, 32:40, :].astype(F32)
            left = [[] for _ in range(N_GY)]
            right = []
            for c in range(CAP):
                base = pl.multiple_of(owner * (CAP * SHARE) + c * SHARE, SHARE)
                v = turned_ref[pl.ds(base, SHARE), :]
                twice = jnp.concatenate([v, v], axis=0).astype(BF)
                row = jnp.broadcast_to(codes[c : c + 1, :], (2 * SHARE, DEV)).astype(BF)
                pair = row - half_iota
                for k in range(CY // 2):
                    left[k].append(jnp.where(pair == jnp.asarray(2 * k, BF), twice, zero))
                col = jnp.broadcast_to(codes[CAP + c : CAP + c + 1, :], (CX, DEV)).astype(BF)
                right.append(jnp.where(col == col_iota, one, zero))
            lhs = jnp.concatenate([jnp.concatenate(x, axis=1) for x in left], axis=0)
            rhs = jnp.concatenate(right, axis=1)
            dense = dot(lhs, rhs, ((1,), (1,)))
            dense_ref[b * 128 : (b + 1) * 128, :] = dense.astype(BF)
        gain = dot(dense_ref[...], kx_vmem[pl.ds(pl.multiple_of(step * CX, CX), CX), :])
        for h in range(2):
            acc_ref[h * 1024 : (h + 1) * 1024, :] += gain[:, h * 128 : (h + 1) * 128]
        return carry

    lax.fori_loop(0, N_GX, column_block, 0)
    for l in range(SHARE):
        along_x = jnp.concatenate(
            [acc_ref[pl.ds(h * 1024 + l, NY, stride=SHARE), :] for h in range(2)], axis=1
        ).astype(BF)
        along_y = dot(ky_ref[tracer_ref[0]], along_x, ((0,), (0,))).astype(BF)
        along_ref[l] = along_y
    mine = tracer_ref[1]
    for k in range(N_GY):
        row = pl.multiple_of((mine ^ k) * CY, CY)
        out_refs[k][...] = along_ref[:, pl.ds(row, CY), :]


def smooth_call(tracer, got, inverse_x, inverse_y):
    vmem = pl.BlockSpec(memory_space=pltpu.VMEM)
    return pl.pallas_call(
        smooth_kernel,
        out_shape=[pltpu.VMEM((SHARE, CY, CX), BF)] * N_GY,
        in_specs=[
            pl.BlockSpec(memory_space=pltpu.SMEM),
            vmem,
            pl.BlockSpec(memory_space=pl.ANY),
            vmem,
        ],
        out_specs=[vmem] * N_GY,
        scratch_shapes=[
            pltpu.VMEM((DEV * 32, DEV), F32),
            pltpu.VMEM((SLOTS * SHARE, DEV), F32),
            pltpu.VMEM((NY * SHARE, CX), BF),
            pltpu.VMEM((2 * NY * SHARE, 128), F32),
            pltpu.VMEM((SHARE, NY, CX), BF),
            pltpu.VMEM((N_GX * CX, CX), BF),
            pltpu.SemaphoreType.DMA(()),
        ],
        name="smooth",
    )(tracer, got, inverse_x, inverse_y)


def coef_kernel(coef_ref, inv_ref, gain_ref, ratio_ref):
    ratio = None
    for k in range(LEV):
        here = coef_ref[k]
        below = coef_ref[k + 1] if k + 1 < LEV else jnp.zeros_like(here)
        diagonal = 1.0 + here + below
        if k > 0:
            diagonal = diagonal + here * ratio
        inv = 1.0 / diagonal
        ratio = -below * inv
        inv_ref[k] = inv
        gain_ref[k] = here * inv
        ratio_ref[k] = ratio


def solve_kernel(where_ref, *refs):
    parts = refs[:N_GY]
    inv_ref, gain_ref, ratio_ref, mask_ref, col_ref, inc_ref, pick_ref, field_ref, part_ref = refs[N_GY:]
    mine = where_ref[1]
    for k in range(N_GY):
        field_ref[pl.ds((mine ^ k) * SHARE, SHARE)] = parts[k][...]
    mask = mask_ref[...].astype(F32)
    prev0 = prev1 = None
    for k in range(LEV):
        f0 = field_ref[k].astype(F32) * inv_ref[k]
        f1 = field_ref[LEV + k].astype(F32) * inv_ref[k]
        if k == 0:
            prev0, prev1 = f0, f1
        else:
            prev0 = f0 + gain_ref[k] * prev0
            prev1 = f1 + gain_ref[k] * prev1
        part_ref[k] = prev0
        part_ref[LEV + k] = prev1
    x0, x1 = prev0, prev1
    for k in range(LEV - 1, -1, -1):
        if k < LEV - 1:
            x0 = part_ref[k] - ratio_ref[k] * x0
            x1 = part_ref[LEV + k] - ratio_ref[k] * x1
        inc_ref[k] = (x0 * mask).astype(BF)
        inc_ref[LEV + k] = (x1 * mask).astype(BF)
    cells = col_ref[...]
    row = cells // CX
    col = cells % CX
    packed = jnp.concatenate([row.astype(F32), col.astype(F32)] + [jnp.zeros((6, SLOTS), F32)], axis=0).astype(BF)
    source = iota((SLOTS, SLOTS), 0)
    target = iota((SLOTS, SLOTS), 1)
    moved = dot(packed, one_hot((source % CAP) * DEV + source // CAP == target))
    row = moved[0:1, :].astype(I32)
    col = moved[1:2, :].astype(I32)
    pick_col = one_hot(iota((CX, SLOTS), 0) == col)
    row_iota = iota((LAYERS * CY, SLOTS), 0) % CY
    found = dot(inc_ref[...].reshape(LAYERS * CY, CX), pick_col)
    chosen = jnp.where(row_iota == row, found, 0.0).astype(BF)
    total = one_hot(iota((LAYERS, LAYERS * CY), 1) // CY == iota((LAYERS, LAYERS * CY), 0))
    picked = dot(chosen, total, ((0,), (1,))).astype(BF)
    for r in range(2):
        pair = [picked[(2 * r + h) * DEV : (2 * r + h + 1) * DEV, :] for h in range(2)]
        pick_ref[:, r, :] = jnp.concatenate(pair, axis=1)


def in_vmem(x):
    return pltpu.with_memory_space_constraint(x, pltpu.VMEM)


def call(kernel, out_shape, n_in, name, scratch=()):
    return pl.pallas_call(
        kernel,
        out_shape=out_shape,
        in_specs=[pl.BlockSpec(memory_space=pltpu.VMEM)] * n_in,
        out_specs=jax.tree.map(lambda _: pl.BlockSpec(memory_space=pltpu.VMEM), out_shape),
        scratch_shapes=list(scratch),
        name=name,
    )


def body(innovations, station_columns, profile_counts, land_mask, vertical_coef, inverse_x, inverse_y):
    everyone = ("gx", "gy")
    message = call(send_kernel, pltpu.VMEM((DEV, ROWS, DEV), BF), 4, "send")(
        innovations, station_columns, profile_counts, land_mask
    )
    got = lax.all_to_all(message, everyone, split_axis=0, concat_axis=0, tiled=True)
    mine = lax.axis_index("gy").astype(I32)
    where = jnp.stack([mine * SHARE // LEV, mine])
    products = smooth_call(where, in_vmem(got), inverse_x, inverse_y)
    parts = [products[0]] + [
        lax.ppermute(products[k], "gy", [(i, i ^ k) for i in range(N_GY)]) for k in range(1, N_GY)
    ]
    plane = pltpu.VMEM((LEV, CY, CX), F32)
    inv, gain, ratio = call(coef_kernel, (plane, plane, plane), 1, "coef")(vertical_coef)
    vmem = pl.BlockSpec(memory_space=pltpu.VMEM)
    increment, picked = pl.pallas_call(
        solve_kernel,
        out_shape=(jax.ShapeDtypeStruct((LAYERS, CY, CX), BF), pltpu.VMEM((DEV, 2, DEV), BF)),
        in_specs=[pl.BlockSpec(memory_space=pltpu.SMEM)] + [vmem] * (N_GY + 5),
        out_specs=(vmem, vmem),
        scratch_shapes=[pltpu.VMEM((LAYERS, CY, CX), BF), pltpu.VMEM((LAYERS, CY, CX), F32)],
        name="solve",
    )(where, *[in_vmem(p) for p in parts], in_vmem(inv), in_vmem(gain), in_vmem(ratio), land_mask, station_columns)
    returned = lax.all_to_all(picked, everyone, split_axis=0, concat_axis=0, tiled=True)
    returned = returned.reshape(SLOTS, LAYERS).T.reshape(1, LAYERS, SLOTS)
    slot_index = lax.broadcasted_iota(I32, (DEV, CAP), 1)
    live = (slot_index < profile_counts[0][:, None]).reshape(SLOTS)
    equivalents = jnp.where(live[None, None, :], returned, jnp.zeros((), BF))
    return increment, equivalents


def solution(mesh):
    in_specs = (
        P(("gx", "gy"), None, None),
        P(("gx", "gy"), None),
        P(("gx", "gy"), None),
        P("gy", "gx"),
        P(None, "gy", "gx"),
        P(None, None, "gx"),
        P(),
    )
    out_specs = (P(None, "gy", "gx"), P(("gx", "gy"), None, None))
    return jax.shard_map(body, mesh=mesh, in_specs=in_specs, out_specs=out_specs, check_vma=False)
```

```python
import functools
import jax
import jax.numpy as jnp
from jax import lax
from jax.experimental import pallas as pl
from jax.experimental.pallas import tpu as pltpu
from jax.sharding import PartitionSpec as P

LEV = 32
CAP = 4
CY = 16
CX = 256
LAYERS = 64
NY = 128
N_GX = 16
N_GY = 8
DEV = 128
SLOTS = DEV * CAP
SHARE = LAYERS // N_GY
ROWS = 40
BF = jnp.bfloat16
F32 = jnp.float32
I32 = jnp.int32


def iota(shape, dim):
    return lax.broadcasted_iota(I32, shape, dim)


def one_hot(cond):
    return jnp.where(cond, 1.0, 0.0).astype(BF)


def dot(a, b, dims=((1,), (0,))):
    return lax.dot_general(a, b, (dims, ((), ())), preferred_element_type=F32)


def send_kernel(inn_ref, col_ref, cnt_ref, mask_ref, out_ref):
    counts = jnp.broadcast_to(cnt_ref[...], (8, DEV)).astype(F32).astype(BF)
    spread = one_hot(iota((DEV, SLOTS), 1) // CAP == iota((DEV, SLOTS), 0))
    count_lane = dot(counts, spread)[0:1, :]
    slot_lane = (iota((1, SLOTS), 1) % CAP).astype(F32)
    live = slot_lane < count_lane
    values = jnp.where(live, inn_ref[0].astype(F32), 0.0).astype(BF)
    cells = col_ref[...]
    row = cells // CX
    col = cells % CX
    pick_col = one_hot(iota((CX, SLOTS), 0) == col)
    sea_rows = dot(mask_ref[...].astype(F32).astype(BF), pick_col)
    sea = jnp.sum(jnp.where(iota((CY, SLOTS), 0) == row, sea_rows, 0.0), axis=0, keepdims=True)
    row_code = jnp.where(sea > 0.5, row.astype(F32), 255.0)
    codes = jnp.where(
        iota((8, SLOTS), 0) == 0,
        jnp.broadcast_to(row_code, (8, SLOTS)),
        jnp.broadcast_to(col.astype(F32), (8, SLOTS)),
    ).astype(BF)
    source = iota((SLOTS, SLOTS), 0)
    target = iota((SLOTS, SLOTS), 1)
    permute = one_hot((source % CAP) * DEV + source // CAP == target)
    moved = dot(codes, permute)
    tile = jnp.concatenate(
        [moved[0:1, c * DEV : (c + 1) * DEV] for c in range(CAP)]
        + [moved[1:2, c * DEV : (c + 1) * DEV] for c in range(CAP)],
        axis=0,
    ).astype(BF)
    for b in range(N_GY):
        block = values[b * SHARE : (b + 1) * SHARE, :]
        message = jnp.concatenate(
            [block[:, q * DEV : (q + 1) * DEV] for q in range(CAP)] + [tile], axis=0
        )
        for a in range(N_GX):
            out_ref[a * N_GY + b] = message


def smooth_kernel(
    tracer_ref, got_ref, kx_ref, ky_ref, *refs
):
    out_refs = refs[:N_GY]
    wide_ref, turned_ref, column_ref, dense_ref, acc_ref, along_ref, kx_vmem, sem = refs[N_GY:]
    fetch = pltpu.make_async_copy(kx_ref.at[tracer_ref[0]], kx_vmem, sem)
    fetch.start()
    acc_ref[...] = jnp.zeros_like(acc_ref)

    def widen(s, carry):
        wide_ref[pl.ds(pl.multiple_of(s * ROWS, 8), ROWS), :] = got_ref[s].astype(F32)
        return carry

    lax.fori_loop(0, DEV, widen, 0, unroll=8)
    for q in range(CAP):
        for l in range(SHARE):
            block = wide_ref[pl.ds(q * SHARE + l, DEV, stride=ROWS), :]
            turned_ref[pl.ds(q * DEV * SHARE + l, DEV, stride=SHARE), :] = block.T
    for c in range(CAP):
        column_ref[c] = wide_ref[pl.ds(36 + c, DEV, stride=ROWS), :].T
    fetch.wait()

    col_iota = [(iota((DEV, DEV), 1) + h * DEV).astype(F32).astype(BF) for h in range(2)]
    half_iota = (iota((2 * SHARE, DEV), 0) // SHARE).astype(F32).astype(BF)
    zero = jnp.zeros((), BF)
    one = jnp.ones((), BF)

    def column_block(step, carry):
        for b in range(N_GY):
            owner = step * N_GY + b
            codes = got_ref[owner, 32:40, :].astype(F32)
            left = [[] for _ in range(N_GY)]
            right = []
            for c in range(CAP):
                base = pl.multiple_of(owner * (CAP * SHARE) + c * SHARE, SHARE)
                v = turned_ref[pl.ds(base, SHARE), :]
                twice = jnp.concatenate([v, v], axis=0).astype(BF)
                row = jnp.broadcast_to(codes[c : c + 1, :], (2 * SHARE, DEV)).astype(BF)
                pair = row - half_iota
                for k in range(CY // 2):
                    left[k].append(jnp.where(pair == jnp.asarray(2 * k, BF), twice, zero))
                col = jnp.take_along_axis(column_ref[c], jnp.full((DEV, DEV), owner, I32), axis=1).astype(BF)
                right.append(jnp.concatenate([jnp.where(col == x, one, zero) for x in col_iota], axis=1))
            lhs = jnp.concatenate([jnp.concatenate(x, axis=1) for x in left], axis=0)
            rhs = jnp.concatenate(right, axis=0)
            dense = dot(lhs, rhs)
            dense_ref[b * 128 : (b + 1) * 128, :] = dense.astype(BF)
        gain = dot(dense_ref[...], kx_vmem[pl.ds(pl.multiple_of(step * CX, CX), CX), :])
        for h in range(2):
            acc_ref[h * 1024 : (h + 1) * 1024, :] += gain[:, h * 128 : (h + 1) * 128]
        return carry

    lax.fori_loop(0, N_GX, column_block, 0, unroll=16)
    for l in range(SHARE):
        along_x = jnp.concatenate(
            [acc_ref[pl.ds(h * 1024 + l, NY, stride=SHARE), :] for h in range(2)], axis=1
        ).astype(BF)
        along_y = dot(ky_ref[tracer_ref[0]], along_x, ((0,), (0,))).astype(BF)
        along_ref[l] = along_y
    mine = tracer_ref[1]
    for k in range(N_GY):
        row = pl.multiple_of((mine ^ k) * CY, CY)
        out_refs[k][...] = along_ref[:, pl.ds(row, CY), :]


def smooth_call(tracer, got, inverse_x, inverse_y):
    vmem = pl.BlockSpec(memory_space=pltpu.VMEM)
    return pl.pallas_call(
        smooth_kernel,
        out_shape=[pltpu.VMEM((SHARE, CY, CX), BF)] * N_GY,
        in_specs=[
            pl.BlockSpec(memory_space=pltpu.SMEM),
            vmem,
            pl.BlockSpec(memory_space=pl.ANY),
            vmem,
        ],
        out_specs=[vmem] * N_GY,
        scratch_shapes=[
            pltpu.VMEM((DEV * ROWS, DEV), F32),
            pltpu.VMEM((SLOTS * SHARE, DEV), F32),
            pltpu.VMEM((CAP, DEV, DEV), F32),
            pltpu.VMEM((NY * SHARE, CX), BF),
            pltpu.VMEM((2 * NY * SHARE, 128), F32),
            pltpu.VMEM((SHARE, NY, CX), BF),
            pltpu.VMEM((N_GX * CX, CX), BF),
            pltpu.SemaphoreType.DMA(()),
        ],
        name="smooth",
    )(tracer, got, inverse_x, inverse_y)


def coef_kernel(coef_ref, inv_ref, gain_ref, ratio_ref):
    ratio = None
    for k in range(LEV):
        here = coef_ref[k]
        below = coef_ref[k + 1] if k + 1 < LEV else jnp.zeros_like(here)
        diagonal = 1.0 + here + below
        if k > 0:
            diagonal = diagonal + here * ratio
        inv = 1.0 / diagonal
        ratio = -below * inv
        inv_ref[k] = inv
        gain_ref[k] = here * inv
        ratio_ref[k] = ratio


def solve_kernel(where_ref, *refs):
    parts = refs[:N_GY]
    inv_ref, gain_ref, ratio_ref, mask_ref, col_ref, inc_ref, pick_ref, field_ref, part_ref = refs[N_GY:]
    mine = where_ref[1]
    for k in range(N_GY):
        field_ref[pl.ds((mine ^ k) * SHARE, SHARE)] = parts[k][...]
    mask = mask_ref[...].astype(F32)
    prev0 = prev1 = None
    for k in range(LEV):
        f0 = field_ref[k].astype(F32) * inv_ref[k]
        f1 = field_ref[LEV + k].astype(F32) * inv_ref[k]
        if k == 0:
            prev0, prev1 = f0, f1
        else:
            prev0 = f0 + gain_ref[k] * prev0
            prev1 = f1 + gain_ref[k] * prev1
        part_ref[k] = prev0
        part_ref[LEV + k] = prev1
    x0, x1 = prev0, prev1
    for k in range(LEV - 1, -1, -1):
        if k < LEV - 1:
            x0 = part_ref[k] - ratio_ref[k] * x0
            x1 = part_ref[LEV + k] - ratio_ref[k] * x1
        inc_ref[k] = (x0 * mask).astype(BF)
        inc_ref[LEV + k] = (x1 * mask).astype(BF)
    cells = col_ref[...]
    row = cells // CX
    col = cells % CX
    packed = jnp.concatenate([row.astype(F32), col.astype(F32)] + [jnp.zeros((6, SLOTS), F32)], axis=0).astype(BF)
    source = iota((SLOTS, SLOTS), 0)
    target = iota((SLOTS, SLOTS), 1)
    moved = dot(packed, one_hot((source % CAP) * DEV + source // CAP == target))
    row = moved[0:1, :].astype(I32)
    col = moved[1:2, :].astype(I32)
    pick_col = one_hot(iota((CX, SLOTS), 0) == col)
    row_iota = iota((LAYERS * CY, SLOTS), 0) % CY
    found = dot(inc_ref[...].reshape(LAYERS * CY, CX), pick_col)
    chosen = jnp.where(row_iota == row, found, 0.0).astype(BF)
    total = one_hot(iota((LAYERS, LAYERS * CY), 1) // CY == iota((LAYERS, LAYERS * CY), 0))
    picked = dot(chosen, total, ((0,), (1,))).astype(BF)
    for r in range(2):
        pair = [picked[(2 * r + h) * DEV : (2 * r + h + 1) * DEV, :] for h in range(2)]
        pick_ref[:, r, :] = jnp.concatenate(pair, axis=1)


def in_vmem(x):
    return pltpu.with_memory_space_constraint(x, pltpu.VMEM)


def call(kernel, out_shape, n_in, name, scratch=()):
    return pl.pallas_call(
        kernel,
        out_shape=out_shape,
        in_specs=[pl.BlockSpec(memory_space=pltpu.VMEM)] * n_in,
        out_specs=jax.tree.map(lambda _: pl.BlockSpec(memory_space=pltpu.VMEM), out_shape),
        scratch_shapes=list(scratch),
        name=name,
    )


def body(innovations, station_columns, profile_counts, land_mask, vertical_coef, inverse_x, inverse_y):
    everyone = ("gx", "gy")
    message = call(send_kernel, pltpu.VMEM((DEV, ROWS, DEV), BF), 4, "send")(
        innovations, station_columns, profile_counts, land_mask
    )
    got = lax.all_to_all(message, everyone, split_axis=0, concat_axis=0, tiled=True)
    mine = lax.axis_index("gy").astype(I32)
    where = jnp.stack([mine * SHARE // LEV, mine])
    products = smooth_call(where, in_vmem(got), inverse_x, inverse_y)
    parts = [products[0]] + [
        lax.ppermute(products[k], "gy", [(i, i ^ k) for i in range(N_GY)]) for k in range(1, N_GY)
    ]
    plane = pltpu.VMEM((LEV, CY, CX), F32)
    inv, gain, ratio = call(coef_kernel, (plane, plane, plane), 1, "coef")(vertical_coef)
    vmem = pl.BlockSpec(memory_space=pltpu.VMEM)
    increment, picked = pl.pallas_call(
        solve_kernel,
        out_shape=(jax.ShapeDtypeStruct((LAYERS, CY, CX), BF), pltpu.VMEM((DEV, 2, DEV), BF)),
        in_specs=[pl.BlockSpec(memory_space=pltpu.SMEM)] + [vmem] * (N_GY + 5),
        out_specs=(vmem, vmem),
        scratch_shapes=[pltpu.VMEM((LAYERS, CY, CX), BF), pltpu.VMEM((LAYERS, CY, CX), F32)],
        name="solve",
    )(where, *[in_vmem(p) for p in parts], in_vmem(inv), in_vmem(gain), in_vmem(ratio), land_mask, station_columns)
    returned = lax.all_to_all(picked, everyone, split_axis=0, concat_axis=0, tiled=True)
    returned = returned.reshape(SLOTS, LAYERS).T.reshape(1, LAYERS, SLOTS)
    slot_index = lax.broadcasted_iota(I32, (DEV, CAP), 1)
    live = (slot_index < profile_counts[0][:, None]).reshape(SLOTS)
    equivalents = jnp.where(live[None, None, :], returned, jnp.zeros((), BF))
    return increment, equivalents


def solution(mesh):
    in_specs = (
        P(("gx", "gy"), None, None),
        P(("gx", "gy"), None),
        P(("gx", "gy"), None),
        P("gy", "gx"),
        P(None, "gy", "gx"),
        P(None, None, "gx"),
        P(),
    )
    out_specs = (P(None, "gy", "gx"), P(("gx", "gy"), None, None))
    return jax.shard_map(body, mesh=mesh, in_specs=in_specs, out_specs=out_specs, check_vma=False)
```

```python
import functools
import jax
import jax.numpy as jnp
from jax import lax
from jax.experimental import pallas as pl
from jax.experimental.pallas import tpu as pltpu
from jax.sharding import PartitionSpec as P

LEV = 32
CAP = 4
CY = 16
CX = 256
LAYERS = 64
NY = 128
N_GX = 16
N_GY = 8
DEV = 128
SLOTS = DEV * CAP
SHARE = LAYERS // N_GY
ROWS = 40
ORDER = (4, 5, 6, 7, 2, 3, 1, 0)
BF = jnp.bfloat16
F32 = jnp.float32
I32 = jnp.int32


def iota(shape, dim):
    return lax.broadcasted_iota(I32, shape, dim)


def one_hot(cond):
    return jnp.where(cond, 1.0, 0.0).astype(BF)


def dot(a, b, dims=((1,), (0,))):
    return lax.dot_general(a, b, (dims, ((), ())), preferred_element_type=F32)


def send_kernel(inn_ref, col_ref, cnt_ref, mask_ref, out_ref, code_ref, message_ref, sems):
    counts = jnp.broadcast_to(cnt_ref[...], (8, DEV)).astype(F32).astype(BF)
    spread = one_hot(iota((DEV, SLOTS), 1) // CAP == iota((DEV, SLOTS), 0))
    count_lane = dot(counts, spread)[0:1, :]
    slot_lane = (iota((1, SLOTS), 1) % CAP).astype(F32)
    live = slot_lane < count_lane
    values = jnp.where(live, inn_ref[0].astype(F32), 0.0).astype(BF)
    cells = col_ref[...]
    row = cells // CX
    col = cells % CX
    pick_col = one_hot(iota((CX, SLOTS), 0) == col)
    sea_rows = dot(mask_ref[...].astype(F32).astype(BF), pick_col)
    sea = jnp.sum(jnp.where(iota((CY, SLOTS), 0) == row, sea_rows, 0.0), axis=0, keepdims=True)
    row_code = jnp.where(sea > 0.5, row.astype(F32), 255.0)
    codes = jnp.where(
        iota((8, SLOTS), 0) == 0,
        jnp.broadcast_to(row_code, (8, SLOTS)),
        jnp.broadcast_to(col.astype(F32), (8, SLOTS)),
    ).astype(BF)
    source = iota((SLOTS, SLOTS), 0)
    target = iota((SLOTS, SLOTS), 1)
    permute = one_hot((source % CAP) * DEV + source // CAP == target)
    moved = dot(codes, permute)
    tile = jnp.concatenate(
        [moved[0:1, c * DEV : (c + 1) * DEV] for c in range(CAP)]
        + [moved[1:2, c * DEV : (c + 1) * DEV] for c in range(CAP)],
        axis=0,
    ).astype(BF)
    code_ref[...] = tile.astype(F32)
    for b in range(N_GY):
        block = values[b * SHARE : (b + 1) * SHARE, :]
        message_ref[b] = jnp.concatenate(
            [block[:, q * DEV : (q + 1) * DEV] for q in range(CAP)] + [tile], axis=0
        )
    copies = [
        pltpu.make_async_copy(message_ref, out_ref.at[pl.ds(a * N_GY, N_GY)], sems.at[a])
        for a in range(N_GX)
    ]
    for copy in copies:
        copy.start()
    for copy in copies:
        copy.wait()


def smooth_kernel(
    tracer_ref, got_ref, kx_ref, ky_ref, *refs
):
    out_refs = refs[:N_GY]
    wide_ref, turned_ref, column_ref, dense_ref, acc_ref, along_ref, kx_vmem, sem = refs[N_GY:]
    fetch = pltpu.make_async_copy(kx_ref.at[tracer_ref[0]], kx_vmem, sem)
    fetch.start()
    acc_ref[...] = jnp.zeros_like(acc_ref)

    def widen(s, carry):
        wide_ref[pl.ds(pl.multiple_of(s * ROWS, 8), ROWS), :] = got_ref[s].astype(F32)
        return carry

    lax.fori_loop(0, DEV, widen, 0, unroll=8)
    for q in range(CAP):
        for l in range(SHARE):
            block = wide_ref[pl.ds(q * SHARE + l, DEV, stride=ROWS), :]
            turned_ref[pl.ds(q * DEV * SHARE + l, DEV, stride=SHARE), :] = block.T
    for c in range(CAP):
        column_ref[c] = wide_ref[pl.ds(36 + c, DEV, stride=ROWS), :].T
    fetch.wait()

    col_iota = [(iota((DEV, DEV), 1) + h * DEV).astype(F32).astype(BF) for h in range(2)]
    half_iota = (iota((2 * SHARE, DEV), 0) // SHARE).astype(F32).astype(BF)
    zero = jnp.zeros((), BF)
    one = jnp.ones((), BF)

    def column_block(step, carry):
        for b in range(N_GY):
            owner = step * N_GY + b
            codes = got_ref[owner, 32:40, :].astype(F32)
            left = [[] for _ in range(N_GY)]
            right = []
            for c in range(CAP):
                base = pl.multiple_of(owner * (CAP * SHARE) + c * SHARE, SHARE)
                v = turned_ref[pl.ds(base, SHARE), :]
                twice = jnp.concatenate([v, v], axis=0).astype(BF)
                row = jnp.broadcast_to(codes[c : c + 1, :], (2 * SHARE, DEV)).astype(BF)
                pair = row - half_iota
                for k in range(CY // 2):
                    left[k].append(jnp.where(pair == jnp.asarray(2 * k, BF), twice, zero))
                col = jnp.take_along_axis(column_ref[c], jnp.full((DEV, DEV), owner, I32), axis=1).astype(BF)
                right.append(jnp.concatenate([jnp.where(col == x, one, zero) for x in col_iota], axis=1))
            lhs = jnp.concatenate([jnp.concatenate(x, axis=1) for x in left], axis=0)
            rhs = jnp.concatenate(right, axis=0)
            dense = dot(lhs, rhs)
            dense_ref[b * 128 : (b + 1) * 128, :] = dense.astype(BF)
        kernel_rows = kx_vmem[pl.ds(pl.multiple_of(step * CX, CX), CX), :]
        for m in range(2):
            gain = dot(dense_ref[m * 512 : (m + 1) * 512, :], kernel_rows)
            for h in range(2):
                acc_ref[h * 1024 + m * 512 : h * 1024 + (m + 1) * 512, :] += gain[:, h * 128 : (h + 1) * 128]
        return carry

    lax.fori_loop(0, N_GX, column_block, 0, unroll=16)
    for l in range(SHARE):
        along_x = jnp.concatenate(
            [acc_ref[pl.ds(h * 1024 + l, NY, stride=SHARE), :] for h in range(2)], axis=1
        ).astype(BF)
        along_y = dot(ky_ref[tracer_ref[0]], along_x, ((0,), (0,))).astype(BF)
        along_ref[l] = along_y
    mine = tracer_ref[1]
    for out_ref, k in zip(out_refs, ORDER):
        row = pl.multiple_of((mine ^ k) * CY, CY)
        out_ref[...] = along_ref[:, pl.ds(row, CY), :]


def smooth_call(tracer, got, inverse_x, inverse_y):
    vmem = pl.BlockSpec(memory_space=pltpu.VMEM)
    return pl.pallas_call(
        smooth_kernel,
        out_shape=[pltpu.VMEM((SHARE, CY, CX), BF)] * N_GY,
        in_specs=[
            pl.BlockSpec(memory_space=pltpu.SMEM),
            vmem,
            pl.BlockSpec(memory_space=pl.ANY),
            vmem,
        ],
        out_specs=[vmem] * N_GY,
        scratch_shapes=[
            pltpu.VMEM((DEV * ROWS, DEV), F32),
            pltpu.VMEM((SLOTS * SHARE, DEV), F32),
            pltpu.VMEM((CAP, DEV, DEV), F32),
            pltpu.VMEM((NY * SHARE, CX), BF),
            pltpu.VMEM((2 * NY * SHARE, 128), F32),
            pltpu.VMEM((SHARE, NY, CX), BF),
            pltpu.VMEM((N_GX * CX, CX), BF),
            pltpu.SemaphoreType.DMA(()),
        ],
        name="smooth",
    )(tracer, got, inverse_x, inverse_y)


def coef_kernel(coef_ref, inv_ref, gain_ref, ratio_ref):
    ratio = None
    for k in range(LEV):
        here = coef_ref[k]
        below = coef_ref[k + 1] if k + 1 < LEV else jnp.zeros_like(here)
        diagonal = 1.0 + here + below
        if k > 0:
            diagonal = diagonal + here * ratio
        inv = 1.0 / diagonal
        ratio = -below * inv
        inv_ref[k] = inv
        gain_ref[k] = here * inv
        ratio_ref[k] = ratio


def solve_kernel(where_ref, *refs):
    parts = refs[:N_GY]
    inv_ref, gain_ref, ratio_ref, mask_ref, code_ref, inc_ref, pick_ref, field_ref, part_ref = refs[N_GY:]
    mine = where_ref[1]
    for part, k in zip(parts, ORDER):
        field_ref[pl.ds((mine ^ k) * SHARE, SHARE)] = part[...]
    mask = mask_ref[...].astype(F32)
    prev0 = prev1 = None
    for k in range(LEV):
        f0 = field_ref[k].astype(F32) * inv_ref[k]
        f1 = field_ref[LEV + k].astype(F32) * inv_ref[k]
        if k == 0:
            prev0, prev1 = f0, f1
        else:
            prev0 = f0 + gain_ref[k] * prev0
            prev1 = f1 + gain_ref[k] * prev1
        part_ref[k] = prev0
        part_ref[LEV + k] = prev1
    x0, x1 = prev0, prev1
    for k in range(LEV - 1, -1, -1):
        if k < LEV - 1:
            x0 = part_ref[k] - ratio_ref[k] * x0
            x1 = part_ref[LEV + k] - ratio_ref[k] * x1
        inc_ref[k] = (x0 * mask).astype(BF)
        inc_ref[LEV + k] = (x1 * mask).astype(BF)
    codes = code_ref[...]
    row = jnp.concatenate([codes[c : c + 1, :] for c in range(CAP)], axis=1).astype(I32)
    col = jnp.concatenate([codes[CAP + c : CAP + c + 1, :] for c in range(CAP)], axis=1).astype(I32)
    pick_col = one_hot(iota((CX, SLOTS), 0) == col)
    found = dot(inc_ref[...].reshape(LAYERS * CY, CX), pick_col)
    chosen = jnp.where(iota((LAYERS * CY, SLOTS), 0) % CY == row, found, 0.0).astype(BF)
    total = one_hot(iota((LAYERS, LAYERS * CY), 1) // CY == iota((LAYERS, LAYERS * CY), 0))
    picked = dot(total, chosen)
    turned = [picked[:, c * DEV : (c + 1) * DEV].T for c in range(CAP)]
    for r in range(2):
        pick_ref[:, r, :] = jnp.concatenate(turned[2 * r : 2 * r + 2], axis=1).astype(BF)


def in_vmem(x):
    return pltpu.with_memory_space_constraint(x, pltpu.VMEM)


def call(kernel, out_shape, n_in, name, scratch=()):
    return pl.pallas_call(
        kernel,
        out_shape=out_shape,
        in_specs=[pl.BlockSpec(memory_space=pltpu.VMEM)] * n_in,
        out_specs=jax.tree.map(lambda _: pl.BlockSpec(memory_space=pltpu.VMEM), out_shape),
        scratch_shapes=list(scratch),
        name=name,
    )


def body(innovations, station_columns, profile_counts, land_mask, vertical_coef, inverse_x, inverse_y):
    everyone = ("gx", "gy")
    vmem = pl.BlockSpec(memory_space=pltpu.VMEM)
    message, codes = pl.pallas_call(
        send_kernel,
        out_shape=(jax.ShapeDtypeStruct((DEV, ROWS, DEV), BF), pltpu.VMEM((2 * CAP, DEV), F32)),
        in_specs=[vmem] * 4,
        out_specs=(pl.BlockSpec(memory_space=pl.ANY), vmem),
        scratch_shapes=[pltpu.VMEM((N_GY, ROWS, DEV), BF), pltpu.SemaphoreType.DMA((N_GX,))],
        name="send",
    )(innovations, station_columns, profile_counts, land_mask)
    got = lax.all_to_all(message, everyone, split_axis=0, concat_axis=0, tiled=True)
    mine = lax.axis_index("gy").astype(I32)
    where = jnp.stack([mine * SHARE // LEV, mine])
    products = smooth_call(where, in_vmem(got), inverse_x, inverse_y)
    parts = [
        lax.ppermute(product, "gy", [(i, i ^ k) for i in range(N_GY)]) if k else product
        for product, k in zip(products, ORDER)
    ]
    plane = pltpu.VMEM((LEV, CY, CX), F32)
    inv, gain, ratio = call(coef_kernel, (plane, plane, plane), 1, "coef")(vertical_coef)
    increment, picked = pl.pallas_call(
        solve_kernel,
        out_shape=(pltpu.VMEM((LAYERS, CY, CX), BF), pltpu.VMEM((DEV, 2, DEV), BF)),
        in_specs=[pl.BlockSpec(memory_space=pltpu.SMEM)] + [vmem] * (N_GY + 5),
        out_specs=(vmem, vmem),
        scratch_shapes=[pltpu.VMEM((LAYERS, CY, CX), BF), pltpu.VMEM((LAYERS, CY, CX), F32)],
        name="solve",
    )(where, *[in_vmem(p) for p in parts], in_vmem(inv), in_vmem(gain), in_vmem(ratio), land_mask, in_vmem(codes))
    returned = lax.all_to_all(picked, everyone, split_axis=0, concat_axis=0, tiled=True)
    returned = returned.reshape(SLOTS, LAYERS).T.reshape(1, LAYERS, SLOTS)
    slot_index = lax.broadcasted_iota(I32, (DEV, CAP), 1)
    live = (slot_index < profile_counts[0][:, None]).reshape(SLOTS)
    equivalents = jnp.where(live[None, None, :], returned, jnp.zeros((), BF))
    return increment, equivalents


def solution(mesh):
    in_specs = (
        P(("gx", "gy"), None, None),
        P(("gx", "gy"), None),
        P(("gx", "gy"), None),
        P("gy", "gx"),
        P(None, "gy", "gx"),
        P(None, None, "gx"),
        P(),
    )
    out_specs = (P(None, "gy", "gx"), P(("gx", "gy"), None, None))
    return jax.shard_map(body, mesh=mesh, in_specs=in_specs, out_specs=out_specs, check_vma=False)
```

```python
import jax
import jax.numpy as jnp
from jax import lax
from jax.experimental import pallas as pl
from jax.experimental.pallas import tpu as pltpu
from jax.sharding import PartitionSpec as P

LEV = 32
CAP = 4
CY = 16
CX = 256
LAYERS = 64
NY = 128
N_GX = 16
N_GY = 8
DEV = 128
SLOTS = DEV * CAP
SHARE = LAYERS // N_GY
ROWS = 40
ORDER = (4, 5, 6, 7, 2, 3, 1, 0)
BF = jnp.bfloat16
F32 = jnp.float32
I32 = jnp.int32


def iota(shape, dim):
    return lax.broadcasted_iota(I32, shape, dim)


def one_hot(cond):
    return jnp.where(cond, 1.0, 0.0).astype(BF)


def dot(a, b, dims=((1,), (0,))):
    return lax.dot_general(a, b, (dims, ((), ())), preferred_element_type=F32)


def by_source():
    source = iota((SLOTS, SLOTS), 0)
    owner = source % DEV
    lane = (owner % N_GY) * 64 + (source // DEV) * N_GX + owner // N_GY
    return one_hot(lane == iota((SLOTS, SLOTS), 1))


def send_kernel(inn_ref, col_ref, cnt_ref, mask_ref, out_ref, code_ref, message_ref, sems):
    counts = jnp.broadcast_to(cnt_ref[...], (8, DEV)).astype(F32).astype(BF)
    spread = one_hot(iota((DEV, SLOTS), 1) // CAP == iota((DEV, SLOTS), 0))
    count_lane = dot(counts, spread)[0:1, :]
    slot_lane = (iota((1, SLOTS), 1) % CAP).astype(F32)
    live = slot_lane < count_lane
    values = jnp.where(live, inn_ref[0].astype(F32), 0.0).astype(BF)
    cells = col_ref[...]
    row = cells // CX
    col = cells % CX
    pick_col = one_hot(iota((CX, SLOTS), 0) == col)
    sea_rows = dot(mask_ref[...].astype(F32).astype(BF), pick_col)
    sea = jnp.sum(jnp.where(iota((CY, SLOTS), 0) == row, sea_rows, 0.0), axis=0, keepdims=True)
    row_code = jnp.where(sea > 0.5, row.astype(F32), 255.0)
    codes = jnp.where(
        iota((8, SLOTS), 0) == 0,
        jnp.broadcast_to(row_code, (8, SLOTS)),
        jnp.broadcast_to(col.astype(F32), (8, SLOTS)),
    ).astype(BF)
    source = iota((SLOTS, SLOTS), 0)
    target = iota((SLOTS, SLOTS), 1)
    permute = one_hot((source % CAP) * DEV + source // CAP == target)
    moved = dot(codes, permute)
    tile = jnp.concatenate(
        [moved[0:1, c * DEV : (c + 1) * DEV] for c in range(CAP)]
        + [moved[1:2, c * DEV : (c + 1) * DEV] for c in range(CAP)],
        axis=0,
    ).astype(BF)
    code_ref[...] = tile.astype(F32)
    for b in range(N_GY):
        block = values[b * SHARE : (b + 1) * SHARE, :]
        message_ref[b] = jnp.concatenate(
            [block[:, q * DEV : (q + 1) * DEV] for q in range(CAP)] + [tile], axis=0
        )
    copies = [
        pltpu.make_async_copy(message_ref, out_ref.at[pl.ds(a * N_GY, N_GY)], sems.at[a])
        for a in range(N_GX)
    ]
    for copy in copies:
        copy.start()
    for copy in copies:
        copy.wait()


def smooth_kernel(
    tracer_ref, got_ref, kx_ref, ky_ref, *refs
):
    out_refs = refs[:N_GY]
    wide_ref, turned_ref, column_ref, dense_ref, acc_ref, along_ref, station_ref, kx_vmem, sem = refs[N_GY:]
    fetch = pltpu.make_async_copy(kx_ref.at[tracer_ref[0]], kx_vmem, sem)
    fetch.start()
    acc_ref[...] = jnp.zeros_like(acc_ref)

    def widen(s, carry):
        wide_ref[pl.ds(pl.multiple_of(s * ROWS, 8), ROWS), :] = got_ref[s].astype(F32)
        return carry

    lax.fori_loop(0, DEV, widen, 0, unroll=8)
    for q in range(CAP):
        for l in range(SHARE):
            block = wide_ref[pl.ds(q * SHARE + l, DEV, stride=ROWS), :]
            turned_ref[pl.ds(q * DEV * SHARE + l, DEV, stride=SHARE), :] = block.T
    for c in range(CAP):
        column_ref[c] = wide_ref[pl.ds(36 + c, DEV, stride=ROWS), :].T
    fetch.wait()

    col_iota = [(iota((DEV, DEV), 1) + h * DEV).astype(F32).astype(BF) for h in range(2)]
    half_iota = (iota((2 * SHARE, DEV), 0) // SHARE).astype(F32).astype(BF)
    zero = jnp.zeros((), BF)
    one = jnp.ones((), BF)

    def column_block(step, carry):
        for b in range(N_GY):
            owner = step * N_GY + b
            codes = got_ref[owner, 32:40, :].astype(F32)
            left = [[] for _ in range(N_GY)]
            right = []
            for c in range(CAP):
                base = pl.multiple_of(owner * (CAP * SHARE) + c * SHARE, SHARE)
                v = turned_ref[pl.ds(base, SHARE), :]
                twice = jnp.concatenate([v, v], axis=0).astype(BF)
                row = jnp.broadcast_to(codes[c : c + 1, :], (2 * SHARE, DEV)).astype(BF)
                pair = row - half_iota
                for k in range(CY // 2):
                    left[k].append(jnp.where(pair == jnp.asarray(2 * k, BF), twice, zero))
                col = jnp.take_along_axis(column_ref[c], jnp.full((DEV, DEV), owner, I32), axis=1).astype(BF)
                right.append(jnp.concatenate([jnp.where(col == x, one, zero) for x in col_iota], axis=1))
            lhs = jnp.concatenate([jnp.concatenate(x, axis=1) for x in left], axis=0)
            rhs = jnp.concatenate(right, axis=0)
            dense = dot(lhs, rhs)
            dense_ref[b * 128 : (b + 1) * 128, :] = dense.astype(BF)
        kernel_rows = kx_vmem[pl.ds(pl.multiple_of(step * CX, CX), CX), :]
        for m in range(2):
            gain = dot(dense_ref[m * 512 : (m + 1) * 512, :], kernel_rows)
            for h in range(2):
                acc_ref[h * 1024 + m * 512 : h * 1024 + (m + 1) * 512, :] += gain[:, h * 128 : (h + 1) * 128]
        return carry

    lax.fori_loop(0, N_GX, column_block, 0, unroll=16)
    for l in range(SHARE):
        along_x = jnp.concatenate(
            [acc_ref[pl.ds(h * 1024 + l, NY, stride=SHARE), :] for h in range(2)], axis=1
        ).astype(BF)
        along_y = dot(ky_ref[tracer_ref[0]], along_x, ((0,), (0,))).astype(BF)
        along_ref[l] = along_y
        for h in range(2):
            acc_ref[pl.ds(h * 1024 + l, NY, stride=SHARE), :] = along_y[:, h * 128 : (h + 1) * 128].astype(F32)
    own = [got_ref[tracer_ref[2] * N_GY + b, 32:40, :].astype(F32) for b in range(N_GY)]
    lines = [jnp.concatenate([x[c : c + 1, :] for c in range(CAP)], axis=1) for x in own]
    lines += [jnp.concatenate([x[CAP + c : CAP + c + 1, :] for c in range(CAP)], axis=1) for x in own]
    moved = dot(jnp.concatenate(lines, axis=0).astype(BF), by_source())
    tall_iota = iota((CX, SLOTS), 0).astype(F32).astype(BF)
    found = []
    for b in range(N_GY):
        field = jnp.concatenate(
            [acc_ref[h * 1024 + b * 128 : h * 1024 + (b + 1) * 128, :] for h in range(2)], axis=1
        ).astype(BF)
        col = jnp.broadcast_to(moved[N_GY + b : N_GY + b + 1, :], (16, SLOTS)).astype(BF)
        hit = jnp.where(jnp.concatenate([col] * (CX // 16), axis=0) == tall_iota, one, zero)
        values = dot(field, hit)
        row = jnp.broadcast_to(moved[b : b + 1, :], (SHARE, SLOTS))
        total = jnp.zeros((SHARE, SLOTS), F32)
        for j in range(CY):
            total = total + jnp.where(row == j, values[j * SHARE : (j + 1) * SHARE, :], 0.0)
        found.append(total)
    for g in range(N_GY):
        line = jnp.concatenate([x[:, g * 64 : (g + 1) * 64] for x in found], axis=1)
        station_ref[g] = jnp.concatenate([line[:, :CX], line[:, CX:]], axis=0).astype(BF)
    mine = tracer_ref[1]
    for out_ref, k in zip(out_refs, ORDER):
        row = pl.multiple_of((mine ^ k) * CY, CY)
        out_ref[0:SHARE] = along_ref[:, pl.ds(row, CY), :]
        out_ref[SHARE] = station_ref[mine ^ k]


def smooth_call(tracer, got, inverse_x, inverse_y):
    vmem = pl.BlockSpec(memory_space=pltpu.VMEM)
    return pl.pallas_call(
        smooth_kernel,
        out_shape=[pltpu.VMEM((SHARE + 1, CY, CX), BF)] * N_GY,
        in_specs=[
            pl.BlockSpec(memory_space=pltpu.SMEM),
            vmem,
            pl.BlockSpec(memory_space=pl.ANY),
            vmem,
        ],
        out_specs=[vmem] * N_GY,
        scratch_shapes=[
            pltpu.VMEM((DEV * ROWS, DEV), F32),
            pltpu.VMEM((SLOTS * SHARE, DEV), F32),
            pltpu.VMEM((CAP, DEV, DEV), F32),
            pltpu.VMEM((NY * SHARE, CX), BF),
            pltpu.VMEM((2 * NY * SHARE, 128), F32),
            pltpu.VMEM((SHARE, NY, CX), BF),
            pltpu.VMEM((N_GY, CY, CX), BF),
            pltpu.VMEM((N_GX * CX, CX), BF),
            pltpu.SemaphoreType.DMA(()),
        ],
        name="smooth",
    )(tracer, got, inverse_x, inverse_y)


def coef_kernel(coef_ref, inv_ref, gain_ref, ratio_ref):
    ratio = None
    for k in range(LEV):
        here = coef_ref[k]
        below = coef_ref[k + 1] if k + 1 < LEV else jnp.zeros_like(here)
        diagonal = 1.0 + here + below
        if k > 0:
            diagonal = diagonal + here * ratio
        inv = 1.0 / diagonal
        ratio = -below * inv
        inv_ref[k] = inv
        gain_ref[k] = here * inv
        ratio_ref[k] = ratio


def solve_kernel(where_ref, *refs):
    parts = refs[:N_GY]
    inv_ref, gain_ref, ratio_ref, mask_ref, _, inc_ref, field_ref, part_ref = refs[N_GY:]
    mine = where_ref[1]
    for part, k in zip(parts, ORDER):
        field_ref[pl.ds((mine ^ k) * SHARE, SHARE)] = part[0:SHARE]
    mask = mask_ref[...].astype(F32)
    prev0 = prev1 = None
    for k in range(LEV):
        f0 = field_ref[k].astype(F32) * inv_ref[k]
        f1 = field_ref[LEV + k].astype(F32) * inv_ref[k]
        if k == 0:
            prev0, prev1 = f0, f1
        else:
            prev0 = f0 + gain_ref[k] * prev0
            prev1 = f1 + gain_ref[k] * prev1
        part_ref[k] = prev0
        part_ref[LEV + k] = prev1
    x0, x1 = prev0, prev1
    for k in range(LEV - 1, -1, -1):
        if k < LEV - 1:
            x0 = part_ref[k] - ratio_ref[k] * x0
            x1 = part_ref[LEV + k] - ratio_ref[k] * x1
        inc_ref[k] = (x0 * mask).astype(BF)
        inc_ref[LEV + k] = (x1 * mask).astype(BF)


def gather_kernel(where_ref, coef_ref, code_ref, *refs):
    out_refs = refs[:N_GY]
    found_ref = refs[N_GY]
    codes = code_ref[...]
    lines = [jnp.concatenate([codes[h * CAP + c : h * CAP + c + 1, :] for c in range(CAP)], axis=1) for h in range(2)]
    moved = dot(jnp.concatenate(lines + [jnp.zeros((6, SLOTS), F32)], axis=0).astype(BF), by_source())
    row = moved[0:1, :].astype(I32)
    hit = one_hot(iota((CX, SLOTS), 0) == moved[1:2, :].astype(I32))
    whole = coef_ref[...].reshape(LEV * CY, CX)
    high = whole.astype(BF)
    rest = whole - high.astype(F32)
    middle = rest.astype(BF)
    low = (rest - middle.astype(F32)).astype(BF)
    values = dot(high, hit) + dot(middle, hit) + dot(low, hit)
    chosen = jnp.where(iota((LEV * CY, SLOTS), 0) % CY == row, values, 0.0)
    lines = jnp.sum(chosen.reshape(LEV, CY, SLOTS), axis=1)
    for g in range(N_GY):
        tile = lines[:, (g // 2) * DEV : (g // 2 + 1) * DEV]
        found_ref[g] = pltpu.roll(tile, 64, 1) if g % 2 else tile
    for out_ref, k in zip(out_refs, ORDER):
        out_ref[...] = found_ref[where_ref[1] ^ k]


def station_coef_kernel(where_ref, *refs):
    parts = refs[:N_GY]
    inv_ref, gain_ref, ratio_ref, stage_ref, coef_ref = refs[N_GY:]
    for part, k in zip(parts, ORDER):
        stage_ref[where_ref[1] ^ k] = part[...]
    low = iota((LEV, DEV), 1) < 64
    for t in range(CAP):
        coef_ref[:, t * DEV : (t + 1) * DEV] = jnp.where(
            low, stage_ref[2 * t], pltpu.roll(stage_ref[2 * t + 1], 64, 1)
        )
    ratio = None
    for k in range(LEV):
        here = coef_ref[k : k + 1, :]
        below = coef_ref[k + 1 : k + 2, :] if k + 1 < LEV else jnp.zeros_like(here)
        diagonal = 1.0 + here + below
        if k > 0:
            diagonal = diagonal + here * ratio
        inv = 1.0 / diagonal
        ratio = -below * inv
        inv_ref[k : k + 1, :] = inv
        gain_ref[k : k + 1, :] = here * inv
        ratio_ref[k : k + 1, :] = ratio


def station_kernel(where_ref, *refs):
    parts = refs[:N_GY]
    inv_ref, gain_ref, ratio_ref, out_ref, field_ref, part_ref, turned_ref = refs[N_GY:]
    for part, k in zip(parts, ORDER):
        start = pl.multiple_of((where_ref[1] ^ k) * SHARE, SHARE)
        both = part[SHARE].astype(F32)
        field_ref[pl.ds(start, SHARE), 0:CX] = both[0:SHARE]
        field_ref[pl.ds(start, SHARE), CX:SLOTS] = both[SHARE:CY]
    prev0 = prev1 = None
    for k in range(LEV):
        inv = inv_ref[k : k + 1, :]
        f0 = field_ref[k : k + 1, :] * inv
        f1 = field_ref[LEV + k : LEV + k + 1, :] * inv
        if k == 0:
            prev0, prev1 = f0, f1
        else:
            gain = gain_ref[k : k + 1, :]
            prev0 = f0 + gain * prev0
            prev1 = f1 + gain * prev1
        part_ref[k : k + 1, :] = prev0
        part_ref[LEV + k : LEV + k + 1, :] = prev1
    x0, x1 = prev0, prev1
    for k in range(LEV - 2, -1, -1):
        ratio = ratio_ref[k : k + 1, :]
        x0 = part_ref[k : k + 1, :] - ratio * x0
        x1 = part_ref[LEV + k : LEV + k + 1, :] - ratio * x1
        part_ref[k : k + 1, :] = x0
        part_ref[LEV + k : LEV + k + 1, :] = x1
    empty = jnp.zeros((DEV - LAYERS, DEV), F32)
    for t in range(CAP):
        tile = jnp.concatenate([part_ref[:, t * DEV : (t + 1) * DEV], empty], axis=0)
        turned_ref[t * DEV : (t + 1) * DEV, :] = tile.T
    left = iota((N_GX, DEV), 1) < LAYERS
    for g in range(N_GX):
        even = turned_ref[pl.ds(g, N_GX, stride=32), :]
        odd = turned_ref[pl.ds(N_GX + g, N_GX, stride=32), :]
        out_ref[g] = jnp.where(left, even, pltpu.roll(odd, 64, 1)).astype(BF)


def in_vmem(x):
    return pltpu.with_memory_space_constraint(x, pltpu.VMEM)


def call(kernel, out_shape, n_in, scratch=()):
    return pl.pallas_call(
        kernel,
        out_shape=out_shape,
        in_specs=[pl.BlockSpec(memory_space=pltpu.VMEM)] * n_in,
        out_specs=jax.tree.map(lambda _: pl.BlockSpec(memory_space=pltpu.VMEM), out_shape),
        scratch_shapes=list(scratch),
    )


def inner(innovations, station_columns, profile_counts, land_mask, vertical_coef, inverse_x, inverse_y):
    everyone = ("gx", "gy")
    vmem = pl.BlockSpec(memory_space=pltpu.VMEM)
    message, codes = pl.pallas_call(
        send_kernel,
        out_shape=(jax.ShapeDtypeStruct((DEV, ROWS, DEV), BF), pltpu.VMEM((2 * CAP, DEV), F32)),
        in_specs=[vmem] * 4,
        out_specs=(pl.BlockSpec(memory_space=pl.ANY), vmem),
        scratch_shapes=[pltpu.VMEM((N_GY, ROWS, DEV), BF), pltpu.SemaphoreType.DMA((N_GX,))],
        name="send",
    )(innovations, station_columns, profile_counts, land_mask)
    got = lax.all_to_all(message, everyone, split_axis=0, concat_axis=0, tiled=True)
    mine = lax.axis_index("gy").astype(I32)
    where = jnp.stack([mine * SHARE // LEV, mine, lax.axis_index("gx").astype(I32)])
    smem = pl.BlockSpec(memory_space=pltpu.SMEM)

    def exchange(parts):
        moved = []
        for part, k in zip(parts, ORDER):
            if k:
                part = lax.ppermute(part, "gy", [(i, i ^ k) for i in range(N_GY)])
            moved.append(in_vmem(part))
        return moved

    station_coefs = exchange(
        pl.pallas_call(
            gather_kernel,
            out_shape=[pltpu.VMEM((LEV, DEV), F32)] * N_GY,
            in_specs=[smem, vmem, vmem],
            out_specs=[vmem] * N_GY,
            scratch_shapes=[pltpu.VMEM((N_GY, LEV, DEV), F32)],
            name="gather",
        )(where, vertical_coef, in_vmem(codes)),
    )
    line = pltpu.VMEM((LEV, SLOTS), F32)
    station_lines = pl.pallas_call(
        station_coef_kernel,
        out_shape=[line] * 3,
        in_specs=[smem] + [vmem] * N_GY,
        out_specs=[vmem] * 3,
        scratch_shapes=[pltpu.VMEM((N_GY, LEV, DEV), F32), pltpu.VMEM((LEV, SLOTS), F32)],
        name="station_coef",
    )(where, *station_coefs)
    product = smooth_call(where, in_vmem(got), inverse_x, inverse_y)
    parts = exchange(product)
    plane = pltpu.VMEM((LEV, CY, CX), F32)
    planes = call(coef_kernel, (plane, plane, plane), 1)(vertical_coef)
    picked = pl.pallas_call(
        station_kernel,
        out_shape=pltpu.VMEM((N_GX, N_GX, DEV), BF),
        in_specs=[smem] + [vmem] * (N_GY + 3),
        out_specs=vmem,
        scratch_shapes=[
            pltpu.VMEM((LAYERS, SLOTS), F32),
            pltpu.VMEM((LAYERS, SLOTS), F32),
            pltpu.VMEM((SLOTS, DEV), F32),
        ],
        name="station",
    )(where, *parts, *[in_vmem(x) for x in station_lines])
    returned = lax.all_to_all(picked, "gx", split_axis=0, concat_axis=0, tiled=True)
    increment = pl.pallas_call(
        solve_kernel,
        out_shape=pltpu.VMEM((LAYERS, CY, CX), BF),
        in_specs=[smem] + [vmem] * (N_GY + 4) + [pl.BlockSpec(memory_space=pl.ANY)],
        out_specs=vmem,
        scratch_shapes=[pltpu.VMEM((LAYERS, CY, CX), BF), pltpu.VMEM((LAYERS, CY, CX), F32)],
        name="solve",
    )(where, *parts, *[in_vmem(x) for x in planes], land_mask, picked)
    returned = returned.reshape(SLOTS, LAYERS).T.reshape(1, LAYERS, SLOTS)
    slot_index = lax.broadcasted_iota(I32, (DEV, CAP), 1)
    live = (slot_index < profile_counts[0][:, None]).reshape(SLOTS)
    equivalents = jnp.where(live[None, None, :], returned, jnp.zeros((), BF))
    return increment, equivalents


def solution(mesh):
    in_specs = (
        P(("gx", "gy"), None, None),
        P(("gx", "gy"), None),
        P(("gx", "gy"), None),
        P("gy", "gx"),
        P(None, "gy", "gx"),
        P(None, None, "gx"),
        P(),
    )
    out_specs = (P(None, "gy", "gx"), P(("gx", "gy"), None, None))
    return jax.shard_map(inner, mesh=mesh, in_specs=in_specs, out_specs=out_specs, check_vma=False)
```

```python
import jax
import jax.numpy as jnp
from jax import lax
from jax.experimental import pallas as pl
from jax.experimental.pallas import tpu as pltpu
from jax.sharding import PartitionSpec as P

LEV = 32
CAP = 4
CY = 16
CX = 256
LAYERS = 64
NY = 128
N_GX = 16
N_GY = 8
DEV = 128
SLOTS = DEV * CAP
SHARE = LAYERS // N_GY
ROWS = 40
ORDER = (4, 5, 6, 7, 2, 3, 1, 0)
BF = jnp.bfloat16
F32 = jnp.float32
I32 = jnp.int32


def iota(shape, dim):
    return lax.broadcasted_iota(I32, shape, dim)


def one_hot(cond):
    return jnp.where(cond, 1.0, 0.0).astype(BF)


def dot(a, b, dims=((1,), (0,))):
    return lax.dot_general(a, b, (dims, ((), ())), preferred_element_type=F32)


def by_source():
    source = iota((SLOTS, DEV), 0)
    lane = (source & 7) * 64 + (source >> 7) * N_GX + ((source >> 3) & 15)
    target = iota((SLOTS, DEV), 1)
    return jnp.concatenate([one_hot(lane - t * DEV == target) for t in range(CAP)], axis=1)


def send_kernel(inn_ref, col_ref, cnt_ref, mask_ref, out_ref, code_ref, message_ref, sems):
    counts = jnp.broadcast_to(cnt_ref[...], (8, DEV)).astype(F32).astype(BF)
    spread = one_hot(iota((DEV, SLOTS), 1) >> 2 == iota((DEV, SLOTS), 0))
    count_lane = dot(counts, spread)[0:1, :]
    slot_lane = (iota((1, SLOTS), 1) & 3).astype(F32)
    live = slot_lane < count_lane
    values = jnp.where(live, inn_ref[0].astype(F32), 0.0).astype(BF)
    cells = col_ref[...]
    row = cells >> 8
    col = cells & 255
    pick_col = one_hot(iota((CX, SLOTS), 0) == col)
    sea_rows = dot(mask_ref[...].astype(F32).astype(BF), pick_col)
    sea = jnp.sum(jnp.where(iota((CY, SLOTS), 0) == row, sea_rows, 0.0), axis=0, keepdims=True)
    row_code = jnp.where(sea > 0.5, row.astype(F32), 255.0)
    codes = jnp.where(
        iota((8, SLOTS), 0) == 0,
        jnp.broadcast_to(row_code, (8, SLOTS)),
        jnp.broadcast_to(col.astype(F32), (8, SLOTS)),
    ).astype(BF)
    source = iota((SLOTS, DEV), 0)
    lane = (source & 3) * DEV + (source >> 2)
    target = iota((SLOTS, DEV), 1)
    permute = jnp.concatenate([one_hot(lane - t * DEV == target) for t in range(CAP)], axis=1)
    moved = dot(codes, permute)
    tile = jnp.concatenate(
        [moved[0:1, c * DEV : (c + 1) * DEV] for c in range(CAP)]
        + [moved[1:2, c * DEV : (c + 1) * DEV] for c in range(CAP)],
        axis=0,
    ).astype(BF)
    code_ref[...] = tile.astype(F32)
    for b in range(N_GY):
        block = values[b * SHARE : (b + 1) * SHARE, :]
        message_ref[b] = jnp.concatenate(
            [block[:, q * DEV : (q + 1) * DEV] for q in range(CAP)] + [tile], axis=0
        )
    copies = [
        pltpu.make_async_copy(message_ref, out_ref.at[pl.ds(a * N_GY, N_GY)], sems.at[a])
        for a in range(N_GX)
    ]
    for copy in copies:
        copy.start()
    for copy in copies:
        copy.wait()


def smooth_kernel(
    got_ref, kx_ref, ky_ref, *refs
):
    tracer = lax.axis_index("gy") * SHARE // LEV
    out_refs = refs[:N_GY]
    wide_ref, turned_ref, column_ref, dense_ref, acc_ref, along_ref, station_ref, kx_vmem, sem = refs[N_GY:]
    fetch = pltpu.make_async_copy(kx_ref.at[tracer], kx_vmem, sem)
    fetch.start()
    acc_ref[...] = jnp.zeros_like(acc_ref)

    def widen(s, carry):
        wide_ref[pl.ds(pl.multiple_of(s * ROWS, 8), ROWS), :] = got_ref[s].astype(F32)
        return carry

    lax.fori_loop(0, DEV, widen, 0, unroll=8)
    for q in range(CAP):
        for l in range(SHARE):
            block = wide_ref[pl.ds(q * SHARE + l, DEV, stride=ROWS), :]
            turned_ref[pl.ds(q * DEV * SHARE + l, DEV, stride=SHARE), :] = block.T
    for c in range(CAP):
        column_ref[c] = wide_ref[pl.ds(36 + c, DEV, stride=ROWS), :].T
    fetch.wait()

    col_iota = [(iota((DEV, DEV), 1) + h * DEV).astype(F32).astype(BF) for h in range(2)]
    half_iota = (iota((2 * SHARE, DEV), 0) // SHARE).astype(F32).astype(BF)
    zero = jnp.zeros((), BF)
    one = jnp.ones((), BF)

    def column_block(step, carry):
        for b in range(N_GY):
            owner = step * N_GY + b
            codes = got_ref[owner, 32:40, :].astype(F32)
            left = [[] for _ in range(N_GY)]
            right = []
            for c in range(CAP):
                base = pl.multiple_of(owner * (CAP * SHARE) + c * SHARE, SHARE)
                v = turned_ref[pl.ds(base, SHARE), :]
                twice = jnp.concatenate([v, v], axis=0).astype(BF)
                row = jnp.broadcast_to(codes[c : c + 1, :], (2 * SHARE, DEV)).astype(BF)
                pair = row - half_iota
                for k in range(CY // 2):
                    left[k].append(jnp.where(pair == jnp.asarray(2 * k, BF), twice, zero))
                col = jnp.take_along_axis(column_ref[c], jnp.full((DEV, DEV), owner, I32), axis=1).astype(BF)
                right.append(jnp.concatenate([jnp.where(col == x, one, zero) for x in col_iota], axis=1))
            lhs = jnp.concatenate([jnp.concatenate(x, axis=1) for x in left], axis=0)
            rhs = jnp.concatenate(right, axis=0)
            dense = dot(lhs, rhs)
            dense_ref[b * 128 : (b + 1) * 128, :] = dense.astype(BF)
        kernel_rows = kx_vmem[pl.ds(pl.multiple_of(step * CX, CX), CX), :]
        for m in range(2):
            gain = dot(dense_ref[m * 512 : (m + 1) * 512, :], kernel_rows)
            for h in range(2):
                acc_ref[h * 1024 + m * 512 : h * 1024 + (m + 1) * 512, :] += gain[:, h * 128 : (h + 1) * 128]
        return carry

    lax.fori_loop(0, N_GX, column_block, 0, unroll=16)
    for l in range(SHARE):
        along_x = jnp.concatenate(
            [acc_ref[pl.ds(h * 1024 + l, NY, stride=SHARE), :] for h in range(2)], axis=1
        ).astype(BF)
        along_y = dot(ky_ref[tracer], along_x, ((0,), (0,))).astype(BF)
        along_ref[l] = along_y
        for h in range(2):
            acc_ref[pl.ds(h * 1024 + l, NY, stride=SHARE), :] = along_y[:, h * 128 : (h + 1) * 128].astype(F32)
    own = [got_ref[lax.axis_index("gx") * N_GY + b, 32:40, :].astype(F32) for b in range(N_GY)]
    lines = [jnp.concatenate([x[c : c + 1, :] for c in range(CAP)], axis=1) for x in own]
    lines += [jnp.concatenate([x[CAP + c : CAP + c + 1, :] for c in range(CAP)], axis=1) for x in own]
    moved = dot(jnp.concatenate(lines, axis=0).astype(BF), by_source())
    tall_iota = iota((CX, SLOTS), 0).astype(F32).astype(BF)
    found = []
    for b in range(N_GY):
        field = jnp.concatenate(
            [acc_ref[h * 1024 + b * 128 : h * 1024 + (b + 1) * 128, :] for h in range(2)], axis=1
        ).astype(BF)
        col = jnp.broadcast_to(moved[N_GY + b : N_GY + b + 1, :], (16, SLOTS)).astype(BF)
        hit = jnp.where(jnp.concatenate([col] * (CX // 16), axis=0) == tall_iota, one, zero)
        values = dot(field, hit)
        row = jnp.broadcast_to(moved[b : b + 1, :], (SHARE, SLOTS))
        total = jnp.zeros((SHARE, SLOTS), F32)
        for j in range(CY):
            total = total + jnp.where(row == j, values[j * SHARE : (j + 1) * SHARE, :], 0.0)
        found.append(total)
    for g in range(N_GY):
        line = jnp.concatenate([x[:, g * 64 : (g + 1) * 64] for x in found], axis=1)
        station_ref[g] = jnp.concatenate([line[:, :CX], line[:, CX:]], axis=0).astype(BF)
    mine = lax.axis_index("gy")
    for out_ref, k in zip(out_refs, ORDER):
        row = pl.multiple_of((mine ^ k) * CY, CY)
        out_ref[0:SHARE] = along_ref[:, pl.ds(row, CY), :]
        out_ref[SHARE] = station_ref[mine ^ k]


def smooth_call(got, inverse_x, inverse_y):
    vmem = pl.BlockSpec(memory_space=pltpu.VMEM)
    return pl.pallas_call(
        smooth_kernel,
        out_shape=[pltpu.VMEM((SHARE + 1, CY, CX), BF)] * N_GY,
        in_specs=[
            vmem,
            pl.BlockSpec(memory_space=pl.ANY),
            vmem,
        ],
        out_specs=[vmem] * N_GY,
        scratch_shapes=[
            pltpu.VMEM((DEV * ROWS, DEV), F32),
            pltpu.VMEM((SLOTS * SHARE, DEV), F32),
            pltpu.VMEM((CAP, DEV, DEV), F32),
            pltpu.VMEM((NY * SHARE, CX), BF),
            pltpu.VMEM((2 * NY * SHARE, 128), F32),
            pltpu.VMEM((SHARE, NY, CX), BF),
            pltpu.VMEM((N_GY, CY, CX), BF),
            pltpu.VMEM((N_GX * CX, CX), BF),
            pltpu.SemaphoreType.DMA(()),
        ],
        name="smooth",
    )(got, inverse_x, inverse_y)


def coef_kernel(coef_ref, inv_ref, gain_ref, ratio_ref):
    ratio = None
    for k in range(LEV):
        here = coef_ref[k]
        below = coef_ref[k + 1] if k + 1 < LEV else jnp.zeros_like(here)
        diagonal = 1.0 + here + below
        if k > 0:
            diagonal = diagonal + here * ratio
        inv = 1.0 / diagonal
        ratio = -below * inv
        inv_ref[k] = inv
        gain_ref[k] = here * inv
        ratio_ref[k] = ratio


def solve_kernel(*refs):
    parts = refs[:N_GY]
    inv_ref, gain_ref, ratio_ref, mask_ref, _, inc_ref, field_ref, part_ref = refs[N_GY:]
    mine = lax.axis_index("gy")
    for part, k in zip(parts, ORDER):
        field_ref[pl.ds((mine ^ k) * SHARE, SHARE)] = part[0:SHARE]
    mask = mask_ref[...].astype(F32)
    prev0 = prev1 = None
    for k in range(LEV):
        f0 = field_ref[k].astype(F32) * inv_ref[k]
        f1 = field_ref[LEV + k].astype(F32) * inv_ref[k]
        if k == 0:
            prev0, prev1 = f0, f1
        else:
            prev0 = f0 + gain_ref[k] * prev0
            prev1 = f1 + gain_ref[k] * prev1
        part_ref[k] = prev0
        part_ref[LEV + k] = prev1
    x0, x1 = prev0, prev1
    for k in range(LEV - 1, -1, -1):
        if k < LEV - 1:
            x0 = part_ref[k] - ratio_ref[k] * x0
            x1 = part_ref[LEV + k] - ratio_ref[k] * x1
        inc_ref[k] = (x0 * mask).astype(BF)
        inc_ref[LEV + k] = (x1 * mask).astype(BF)


def gather_kernel(coef_ref, code_ref, *refs):
    out_refs = refs[:N_GY]
    found_ref = refs[N_GY]
    codes = code_ref[...]
    lines = [jnp.concatenate([codes[h * CAP + c : h * CAP + c + 1, :] for c in range(CAP)], axis=1) for h in range(2)]
    moved = dot(jnp.concatenate(lines + [jnp.zeros((6, SLOTS), F32)], axis=0).astype(BF), by_source())
    row = moved[0:1, :].astype(I32)
    hit = one_hot(iota((CX, SLOTS), 0) == moved[1:2, :].astype(I32))
    whole = coef_ref[...].reshape(LEV * CY, CX)
    high = whole.astype(BF)
    rest = whole - high.astype(F32)
    middle = rest.astype(BF)
    low = (rest - middle.astype(F32)).astype(BF)
    values = dot(high, hit) + dot(middle, hit) + dot(low, hit)
    chosen = jnp.where(iota((LEV * CY, SLOTS), 0) % CY == row, values, 0.0)
    lines = jnp.sum(chosen.reshape(LEV, CY, SLOTS), axis=1)
    for g in range(N_GY):
        tile = lines[:, (g // 2) * DEV : (g // 2 + 1) * DEV]
        found_ref[g] = pltpu.roll(tile, 64, 1) if g % 2 else tile
    for out_ref, k in zip(out_refs, ORDER):
        out_ref[...] = found_ref[lax.axis_index("gy") ^ k]


def station_coef_kernel(*refs):
    parts = refs[:N_GY]
    inv_ref, gain_ref, ratio_ref, stage_ref, coef_ref = refs[N_GY:]
    for part, k in zip(parts, ORDER):
        stage_ref[lax.axis_index("gy") ^ k] = part[...]
    low = iota((LEV, DEV), 1) < 64
    for t in range(CAP):
        coef_ref[:, t * DEV : (t + 1) * DEV] = jnp.where(
            low, stage_ref[2 * t], pltpu.roll(stage_ref[2 * t + 1], 64, 1)
        )
    ratio = None
    for k in range(LEV):
        here = coef_ref[k : k + 1, :]
        below = coef_ref[k + 1 : k + 2, :] if k + 1 < LEV else jnp.zeros_like(here)
        diagonal = 1.0 + here + below
        if k > 0:
            diagonal = diagonal + here * ratio
        inv = 1.0 / diagonal
        ratio = -below * inv
        inv_ref[k : k + 1, :] = inv
        gain_ref[k : k + 1, :] = here * inv
        ratio_ref[k : k + 1, :] = ratio


def station_kernel(*refs):
    parts = refs[:N_GY]
    inv_ref, gain_ref, ratio_ref, out_ref, field_ref, part_ref, turned_ref = refs[N_GY:]
    for part, k in zip(parts, ORDER):
        start = pl.multiple_of((lax.axis_index("gy") ^ k) * SHARE, SHARE)
        both = part[SHARE].astype(F32)
        field_ref[pl.ds(start, SHARE), 0:CX] = both[0:SHARE]
        field_ref[pl.ds(start, SHARE), CX:SLOTS] = both[SHARE:CY]
    prev0 = prev1 = None
    for k in range(LEV):
        inv = inv_ref[k : k + 1, :]
        f0 = field_ref[k : k + 1, :] * inv
        f1 = field_ref[LEV + k : LEV + k + 1, :] * inv
        if k == 0:
            prev0, prev1 = f0, f1
        else:
            gain = gain_ref[k : k + 1, :]
            prev0 = f0 + gain * prev0
            prev1 = f1 + gain * prev1
        part_ref[k : k + 1, :] = prev0
        part_ref[LEV + k : LEV + k + 1, :] = prev1
    x0, x1 = prev0, prev1
    for k in range(LEV - 2, -1, -1):
        ratio = ratio_ref[k : k + 1, :]
        x0 = part_ref[k : k + 1, :] - ratio * x0
        x1 = part_ref[LEV + k : LEV + k + 1, :] - ratio * x1
        part_ref[k : k + 1, :] = x0
        part_ref[LEV + k : LEV + k + 1, :] = x1
    empty = jnp.zeros((DEV - LAYERS, DEV), F32)
    for t in range(CAP):
        tile = jnp.concatenate([part_ref[:, t * DEV : (t + 1) * DEV], empty], axis=0)
        turned_ref[t * DEV : (t + 1) * DEV, :] = tile.T
    left = iota((N_GX, DEV), 1) < LAYERS
    for g in range(N_GX):
        even = turned_ref[pl.ds(g, N_GX, stride=32), :]
        odd = turned_ref[pl.ds(N_GX + g, N_GX, stride=32), :]
        out_ref[g] = jnp.where(left, even, pltpu.roll(odd, 64, 1)).astype(BF)


def in_vmem(x):
    return pltpu.with_memory_space_constraint(x, pltpu.VMEM)


def call(kernel, out_shape, n_in, scratch=()):
    return pl.pallas_call(
        kernel,
        out_shape=out_shape,
        in_specs=[pl.BlockSpec(memory_space=pltpu.VMEM)] * n_in,
        out_specs=jax.tree.map(lambda _: pl.BlockSpec(memory_space=pltpu.VMEM), out_shape),
        scratch_shapes=list(scratch),
    )


def inner(innovations, station_columns, profile_counts, land_mask, vertical_coef, inverse_x, inverse_y):
    everyone = ("gx", "gy")
    vmem = pl.BlockSpec(memory_space=pltpu.VMEM)
    message, codes = pl.pallas_call(
        send_kernel,
        out_shape=(jax.ShapeDtypeStruct((DEV, ROWS, DEV), BF), pltpu.VMEM((2 * CAP, DEV), F32)),
        in_specs=[vmem] * 4,
        out_specs=(pl.BlockSpec(memory_space=pl.ANY), vmem),
        scratch_shapes=[pltpu.VMEM((N_GY, ROWS, DEV), BF), pltpu.SemaphoreType.DMA((N_GX,))],
        name="send",
    )(innovations, station_columns, profile_counts, land_mask)
    got = lax.all_to_all(message, everyone, split_axis=0, concat_axis=0, tiled=True)

    def exchange(parts):
        moved = []
        for part, k in zip(parts, ORDER):
            if k:
                part = lax.ppermute(part, "gy", [(i, i ^ k) for i in range(N_GY)])
            moved.append(in_vmem(part))
        return moved

    station_coefs = exchange(
        pl.pallas_call(
            gather_kernel,
            out_shape=[pltpu.VMEM((LEV, DEV), F32)] * N_GY,
            in_specs=[vmem, vmem],
            out_specs=[vmem] * N_GY,
            scratch_shapes=[pltpu.VMEM((N_GY, LEV, DEV), F32)],
            name="gather",
        )(vertical_coef, in_vmem(codes)),
    )
    line = pltpu.VMEM((LEV, SLOTS), F32)
    station_lines = pl.pallas_call(
        station_coef_kernel,
        out_shape=[line] * 3,
        in_specs=[vmem] * N_GY,
        out_specs=[vmem] * 3,
        scratch_shapes=[pltpu.VMEM((N_GY, LEV, DEV), F32), pltpu.VMEM((LEV, SLOTS), F32)],
        name="station_coef",
    )(*station_coefs)
    product = smooth_call(in_vmem(got), inverse_x, inverse_y)
    parts = exchange(product)
    plane = pltpu.VMEM((LEV, CY, CX), F32)
    planes = call(coef_kernel, (plane, plane, plane), 1)(vertical_coef)
    picked = pl.pallas_call(
        station_kernel,
        out_shape=pltpu.VMEM((N_GX, N_GX, DEV), BF),
        in_specs=[vmem] * (N_GY + 3),
        out_specs=vmem,
        scratch_shapes=[
            pltpu.VMEM((LAYERS, SLOTS), F32),
            pltpu.VMEM((LAYERS, SLOTS), F32),
            pltpu.VMEM((SLOTS, DEV), F32),
        ],
        name="station",
    )(*parts, *[in_vmem(x) for x in station_lines])
    returned = lax.all_to_all(picked, "gx", split_axis=0, concat_axis=0, tiled=True)
    increment = pl.pallas_call(
        solve_kernel,
        out_shape=pltpu.VMEM((LAYERS, CY, CX), BF),
        in_specs=[vmem] * (N_GY + 4) + [pl.BlockSpec(memory_space=pl.ANY)],
        out_specs=vmem,
        scratch_shapes=[pltpu.VMEM((LAYERS, CY, CX), BF), pltpu.VMEM((LAYERS, CY, CX), F32)],
        name="solve",
    )(*parts, *[in_vmem(x) for x in planes], land_mask, picked)
    returned = returned.reshape(SLOTS, LAYERS).T.reshape(1, LAYERS, SLOTS)
    slot_index = lax.broadcasted_iota(I32, (DEV, CAP), 1)
    live = (slot_index < profile_counts[0][:, None]).reshape(SLOTS)
    equivalents = jnp.where(live[None, None, :], returned, jnp.zeros((), BF))
    return increment, equivalents


def solution(mesh):
    in_specs = (
        P(("gx", "gy"), None, None),
        P(("gx", "gy"), None),
        P(("gx", "gy"), None),
        P("gy", "gx"),
        P(None, "gy", "gx"),
        P(None, None, "gx"),
        P(),
    )
    out_specs = (P(None, "gy", "gx"), P(("gx", "gy"), None, None))
    return jax.shard_map(inner, mesh=mesh, in_specs=in_specs, out_specs=out_specs, check_vma=False)
```

```python
import jax
import jax.numpy as jnp
from jax import lax
from jax.experimental import pallas as pl
from jax.experimental.pallas import tpu as pltpu
from jax.sharding import PartitionSpec as P

LEV = 32
CAP = 4
CY = 16
CX = 256
LAYERS = 64
NY = 128
N_GX = 16
N_GY = 8
DEV = 128
SLOTS = DEV * CAP
SHARE = LAYERS // N_GY
ROWS = 40
ORDER = (7, 6, 5, 4, 3, 2, 1, 0)
BF = jnp.bfloat16
F32 = jnp.float32
I32 = jnp.int32


def iota(shape, dim):
    return lax.broadcasted_iota(I32, shape, dim)


def one_hot(cond):
    return jnp.where(cond, 1.0, 0.0).astype(BF)


def dot(a, b, dims=((1,), (0,))):
    return lax.dot_general(a, b, (dims, ((), ())), preferred_element_type=F32)


def by_source():
    source = iota((SLOTS, DEV), 0)
    lane = (source & 7) * 64 + (source >> 7) * N_GX + ((source >> 3) & 15)
    target = iota((SLOTS, DEV), 1)
    return jnp.concatenate([one_hot(lane - t * DEV == target) for t in range(CAP)], axis=1)


def send_kernel(inn_ref, col_ref, cnt_ref, mask_ref, out_ref, code_ref, message_ref, sems):
    counts = jnp.broadcast_to(cnt_ref[...], (8, DEV)).astype(F32).astype(BF)
    spread = one_hot(iota((DEV, SLOTS), 1) >> 2 == iota((DEV, SLOTS), 0))
    count_lane = dot(counts, spread)[0:1, :]
    slot_lane = (iota((1, SLOTS), 1) & 3).astype(F32)
    live = slot_lane < count_lane
    values = jnp.where(live, inn_ref[0].astype(F32), 0.0).astype(BF)
    cells = col_ref[...]
    row = cells >> 8
    col = cells & 255
    pick_col = one_hot(iota((CX, SLOTS), 0) == col)
    sea_rows = dot(mask_ref[...].astype(F32).astype(BF), pick_col)
    sea = jnp.sum(jnp.where(iota((CY, SLOTS), 0) == row, sea_rows, 0.0), axis=0, keepdims=True)
    row_code = jnp.where(sea > 0.5, row.astype(F32), 255.0)
    codes = jnp.where(
        iota((8, SLOTS), 0) == 0,
        jnp.broadcast_to(row_code, (8, SLOTS)),
        jnp.broadcast_to(col.astype(F32), (8, SLOTS)),
    ).astype(BF)
    source = iota((SLOTS, DEV), 0)
    lane = (source & 3) * DEV + (source >> 2)
    target = iota((SLOTS, DEV), 1)
    permute = jnp.concatenate([one_hot(lane - t * DEV == target) for t in range(CAP)], axis=1)
    moved = dot(codes, permute)
    tile = jnp.concatenate(
        [moved[0:1, c * DEV : (c + 1) * DEV] for c in range(CAP)]
        + [moved[1:2, c * DEV : (c + 1) * DEV] for c in range(CAP)],
        axis=0,
    ).astype(BF)
    code_ref[...] = tile.astype(F32)
    for b in range(N_GY):
        block = values[b * SHARE : (b + 1) * SHARE, :]
        message_ref[b] = jnp.concatenate(
            [block[:, q * DEV : (q + 1) * DEV] for q in range(CAP)] + [tile], axis=0
        )
    copies = [
        pltpu.make_async_copy(message_ref, out_ref.at[pl.ds(a * N_GY, N_GY)], sems.at[a])
        for a in range(N_GX)
    ]
    for copy in copies:
        copy.start()
    for copy in copies:
        copy.wait()


def smooth_kernel(
    got_ref, kx_ref, ky_ref, *refs
):
    tracer = lax.axis_index("gy") * SHARE // LEV
    out_refs = refs[:N_GY]
    wide_ref, turned_ref, column_ref, dense_ref, acc_ref, along_ref, station_ref, hit_ref, row_ref, kx_vmem, sem = refs[N_GY:]
    fetch = pltpu.make_async_copy(kx_ref.at[tracer], kx_vmem, sem)
    fetch.start()
    acc_ref[...] = jnp.zeros_like(acc_ref)

    def widen(s, carry):
        wide_ref[pl.ds(pl.multiple_of(s * ROWS, 8), ROWS), :] = got_ref[s].astype(F32)
        return carry

    lax.fori_loop(0, DEV, widen, 0, unroll=8)

    def turn(q, l):
        block = wide_ref[pl.ds(q * SHARE + l, DEV, stride=ROWS), :].astype(BF)
        turned_ref[pl.ds(q * DEV * SHARE + l, DEV, stride=SHARE), :] = block.T.astype(F32)

    for q in range(CAP):
        for l in range(SHARE):
            turn(q, l)
    for c in range(CAP):
        column_ref[c] = wide_ref[pl.ds(36 + c, DEV, stride=ROWS), :].T
    own = [got_ref[lax.axis_index("gx") * N_GY + b, 32:40, :].astype(F32) for b in range(N_GY)]
    lines = [jnp.concatenate([x[c : c + 1, :] for c in range(CAP)], axis=1) for x in own]
    lines += [jnp.concatenate([x[CAP + c : CAP + c + 1, :] for c in range(CAP)], axis=1) for x in own]
    moved = dot(jnp.concatenate(lines, axis=0).astype(BF), by_source())
    row_ref[...] = moved[:N_GY, :]
    tall_iota = iota((CX, SLOTS), 0).astype(F32).astype(BF)
    for b in range(N_GY):
        col = jnp.broadcast_to(moved[N_GY + b : N_GY + b + 1, :], (16, SLOTS)).astype(BF)
        hit_ref[b] = jnp.where(
            jnp.concatenate([col] * (CX // 16), axis=0) == tall_iota, jnp.ones((), BF), jnp.zeros((), BF)
        )
    fetch.wait()

    col_iota = [(iota((DEV, DEV), 1) + h * DEV).astype(F32).astype(BF) for h in range(2)]
    half_iota = (iota((2 * SHARE, DEV), 0) // SHARE).astype(F32).astype(BF)
    zero = jnp.zeros((), BF)
    one = jnp.ones((), BF)

    def column_block(step):
        for b in range(N_GY):
            owner = step * N_GY + b
            codes = got_ref[owner, 32:40, :].astype(F32)
            left = [[] for _ in range(N_GY)]
            right = []
            for c in range(CAP):
                base = pl.multiple_of(owner * (CAP * SHARE) + c * SHARE, SHARE)
                v = turned_ref[pl.ds(base, SHARE), :]
                twice = jnp.concatenate([v, v], axis=0).astype(BF)
                row = jnp.broadcast_to(codes[c : c + 1, :], (2 * SHARE, DEV)).astype(BF)
                pair = row - half_iota
                for k in range(CY // 2):
                    left[k].append(jnp.where(pair == jnp.asarray(2 * k, BF), twice, zero))
                col = jnp.take_along_axis(column_ref[c], jnp.full((DEV, DEV), owner, I32), axis=1).astype(BF)
                right.append(jnp.concatenate([jnp.where(col == x, one, zero) for x in col_iota], axis=1))
            lhs = jnp.concatenate([jnp.concatenate(x, axis=1) for x in left], axis=0)
            rhs = jnp.concatenate(right, axis=0)
            dense = dot(lhs, rhs)
            dense_ref[b * 128 : (b + 1) * 128, :] = dense.astype(BF)
        kernel_rows = kx_vmem[pl.ds(pl.multiple_of(step * CX, CX), CX), :]
        for m in range(2):
            gain = dot(dense_ref[m * 512 : (m + 1) * 512, :], kernel_rows)
            for h in range(2):
                acc_ref[h * 1024 + m * 512 : h * 1024 + (m + 1) * 512, :] += gain[:, h * 128 : (h + 1) * 128]

    for step in range(N_GX):
        column_block(step)
    for l in range(SHARE):
        along_x = jnp.concatenate(
            [acc_ref[pl.ds(h * 1024 + l, NY, stride=SHARE), :] for h in range(2)], axis=1
        ).astype(BF)
        along_y = dot(ky_ref[tracer], along_x, ((0,), (0,))).astype(BF)
        along_ref[l] = along_y
        for h in range(2):
            acc_ref[pl.ds(h * 1024 + l, NY, stride=SHARE), :] = along_y[:, h * 128 : (h + 1) * 128].astype(F32)
    found = []
    for b in range(N_GY):
        field = jnp.concatenate(
            [acc_ref[h * 1024 + b * 128 : h * 1024 + (b + 1) * 128, :] for h in range(2)], axis=1
        ).astype(BF)
        values = dot(field, hit_ref[b])
        row = jnp.broadcast_to(row_ref[b : b + 1, :], (SHARE, SLOTS))
        total = jnp.zeros((SHARE, SLOTS), F32)
        for j in range(CY):
            total = total + jnp.where(row == j, values[j * SHARE : (j + 1) * SHARE, :], 0.0)
        found.append(total)
    for g in range(N_GY):
        line = jnp.concatenate([x[:, g * 64 : (g + 1) * 64] for x in found], axis=1)
        station_ref[g] = jnp.concatenate([line[:, :CX], line[:, CX:]], axis=0).astype(BF)
    mine = lax.axis_index("gy")
    for out_ref, k in zip(out_refs, ORDER):
        row = pl.multiple_of((mine ^ k) * CY, CY)
        out_ref[0:SHARE] = along_ref[:, pl.ds(row, CY), :]
        out_ref[SHARE] = station_ref[mine ^ k]


def smooth_call(got, inverse_x, inverse_y):
    vmem = pl.BlockSpec(memory_space=pltpu.VMEM)
    return pl.pallas_call(
        smooth_kernel,
        out_shape=[pltpu.VMEM((SHARE + 1, CY, CX), BF)] * N_GY,
        in_specs=[
            vmem,
            pl.BlockSpec(memory_space=pl.ANY),
            vmem,
        ],
        out_specs=[vmem] * N_GY,
        scratch_shapes=[
            pltpu.VMEM((DEV * ROWS, DEV), F32),
            pltpu.VMEM((SLOTS * SHARE, DEV), F32),
            pltpu.VMEM((CAP, DEV, DEV), F32),
            pltpu.VMEM((NY * SHARE, CX), BF),
            pltpu.VMEM((2 * NY * SHARE, 128), F32),
            pltpu.VMEM((SHARE, NY, CX), BF),
            pltpu.VMEM((N_GY, CY, CX), BF),
            pltpu.VMEM((N_GY, CX, SLOTS), BF),
            pltpu.VMEM((N_GY, SLOTS), F32),
            pltpu.VMEM((N_GX * CX, CX), BF),
            pltpu.SemaphoreType.DMA(()),
        ],
        name="smooth",
    )(got, inverse_x, inverse_y)


def coef_kernel(coef_ref, inv_ref, gain_ref, ratio_ref):
    ratio = None
    for k in range(LEV):
        here = coef_ref[k]
        below = coef_ref[k + 1] if k + 1 < LEV else jnp.zeros_like(here)
        diagonal = 1.0 + here + below
        if k > 0:
            diagonal = diagonal + here * ratio
        inv = 1.0 / diagonal
        ratio = -below * inv
        inv_ref[k] = inv
        gain_ref[k] = here * inv
        ratio_ref[k] = ratio


def solve_kernel(*refs):
    parts = refs[:N_GY]
    inv_ref, gain_ref, ratio_ref, mask_ref, _, inc_ref, field_ref, part_ref = refs[N_GY:]
    mine = lax.axis_index("gy")
    for part, k in zip(parts, ORDER):
        field_ref[pl.ds((mine ^ k) * SHARE, SHARE)] = part[0:SHARE]
    mask = mask_ref[...].astype(F32)
    prev0 = prev1 = None
    for k in range(LEV):
        f0 = field_ref[k].astype(F32) * inv_ref[k]
        f1 = field_ref[LEV + k].astype(F32) * inv_ref[k]
        if k == 0:
            prev0, prev1 = f0, f1
        else:
            prev0 = f0 + gain_ref[k] * prev0
            prev1 = f1 + gain_ref[k] * prev1
        part_ref[k] = prev0
        part_ref[LEV + k] = prev1
    x0, x1 = prev0, prev1
    for k in range(LEV - 1, -1, -1):
        if k < LEV - 1:
            x0 = part_ref[k] - ratio_ref[k] * x0
            x1 = part_ref[LEV + k] - ratio_ref[k] * x1
        inc_ref[k] = (x0 * mask).astype(BF)
        inc_ref[LEV + k] = (x1 * mask).astype(BF)


def gather_kernel(coef_ref, code_ref, *refs):
    out_refs = refs[:N_GY]
    found_ref = refs[N_GY]
    codes = code_ref[...]
    lines = [jnp.concatenate([codes[h * CAP + c : h * CAP + c + 1, :] for c in range(CAP)], axis=1) for h in range(2)]
    moved = dot(jnp.concatenate(lines + [jnp.zeros((6, SLOTS), F32)], axis=0).astype(BF), by_source())
    row = moved[0:1, :].astype(I32)
    hit = one_hot(iota((CX, SLOTS), 0) == moved[1:2, :].astype(I32))
    whole = coef_ref[...].reshape(LEV * CY, CX)
    high = whole.astype(BF)
    rest = whole - high.astype(F32)
    middle = rest.astype(BF)
    low = (rest - middle.astype(F32)).astype(BF)
    values = dot(high, hit) + dot(middle, hit) + dot(low, hit)
    chosen = jnp.where(iota((LEV * CY, SLOTS), 0) % CY == row, values, 0.0)
    lines = jnp.sum(chosen.reshape(LEV, CY, SLOTS), axis=1)
    for g in range(N_GY):
        tile = lines[:, (g // 2) * DEV : (g // 2 + 1) * DEV]
        found_ref[g] = pltpu.roll(tile, 64, 1) if g % 2 else tile
    for out_ref, k in zip(out_refs, ORDER):
        out_ref[...] = found_ref[lax.axis_index("gy") ^ k]


def station_coef_kernel(*refs):
    parts = refs[:N_GY]
    inv_ref, gain_ref, ratio_ref, stage_ref, coef_ref = refs[N_GY:]
    for part, k in zip(parts, ORDER):
        stage_ref[lax.axis_index("gy") ^ k] = part[...]
    low = iota((LEV, DEV), 1) < 64
    for t in range(CAP):
        coef_ref[:, t * DEV : (t + 1) * DEV] = jnp.where(
            low, stage_ref[2 * t], pltpu.roll(stage_ref[2 * t + 1], 64, 1)
        )
    ratio = None
    for k in range(LEV):
        here = coef_ref[k : k + 1, :]
        below = coef_ref[k + 1 : k + 2, :] if k + 1 < LEV else jnp.zeros_like(here)
        diagonal = 1.0 + here + below
        if k > 0:
            diagonal = diagonal + here * ratio
        inv = 1.0 / diagonal
        ratio = -below * inv
        inv_ref[k : k + 1, :] = inv
        gain_ref[k : k + 1, :] = here * inv
        ratio_ref[k : k + 1, :] = ratio


def station_kernel(*refs):
    parts = refs[:N_GY]
    inv_ref, gain_ref, ratio_ref, out_ref, field_ref, part_ref, turned_ref = refs[N_GY:]
    for part, k in zip(parts, ORDER):
        start = pl.multiple_of((lax.axis_index("gy") ^ k) * SHARE, SHARE)
        both = part[SHARE].astype(F32)
        field_ref[pl.ds(start, SHARE), 0:CX] = both[0:SHARE]
        field_ref[pl.ds(start, SHARE), CX:SLOTS] = both[SHARE:CY]
    prev0 = prev1 = None
    for k in range(LEV):
        inv = inv_ref[k : k + 1, :]
        f0 = field_ref[k : k + 1, :] * inv
        f1 = field_ref[LEV + k : LEV + k + 1, :] * inv
        if k == 0:
            prev0, prev1 = f0, f1
        else:
            gain = gain_ref[k : k + 1, :]
            prev0 = f0 + gain * prev0
            prev1 = f1 + gain * prev1
        part_ref[k : k + 1, :] = prev0
        part_ref[LEV + k : LEV + k + 1, :] = prev1
    x0, x1 = prev0, prev1
    for k in range(LEV - 2, -1, -1):
        ratio = ratio_ref[k : k + 1, :]
        x0 = part_ref[k : k + 1, :] - ratio * x0
        x1 = part_ref[LEV + k : LEV + k + 1, :] - ratio * x1
        part_ref[k : k + 1, :] = x0
        part_ref[LEV + k : LEV + k + 1, :] = x1
    empty = jnp.zeros((DEV - LAYERS, DEV), F32)
    for t in range(CAP):
        tile = jnp.concatenate([part_ref[:, t * DEV : (t + 1) * DEV], empty], axis=0)
        turned_ref[t * DEV : (t + 1) * DEV, :] = tile.T
    left = iota((N_GX, DEV), 1) < LAYERS
    for g in range(N_GX):
        even = turned_ref[pl.ds(g, N_GX, stride=32), :]
        odd = turned_ref[pl.ds(N_GX + g, N_GX, stride=32), :]
        out_ref[g] = jnp.where(left, even, pltpu.roll(odd, 64, 1)).astype(BF)


def in_vmem(x):
    return pltpu.with_memory_space_constraint(x, pltpu.VMEM)


def call(kernel, out_shape, n_in, scratch=()):
    return pl.pallas_call(
        kernel,
        out_shape=out_shape,
        in_specs=[pl.BlockSpec(memory_space=pltpu.VMEM)] * n_in,
        out_specs=jax.tree.map(lambda _: pl.BlockSpec(memory_space=pltpu.VMEM), out_shape),
        scratch_shapes=list(scratch),
    )


def inner(innovations, station_columns, profile_counts, land_mask, vertical_coef, inverse_x, inverse_y):
    everyone = ("gx", "gy")
    vmem = pl.BlockSpec(memory_space=pltpu.VMEM)
    message, codes = pl.pallas_call(
        send_kernel,
        out_shape=(jax.ShapeDtypeStruct((DEV, ROWS, DEV), BF), pltpu.VMEM((2 * CAP, DEV), F32)),
        in_specs=[vmem] * 4,
        out_specs=(pl.BlockSpec(memory_space=pl.ANY), vmem),
        scratch_shapes=[pltpu.VMEM((N_GY, ROWS, DEV), BF), pltpu.SemaphoreType.DMA((N_GX,))],
        name="send",
    )(innovations, station_columns, profile_counts, land_mask)
    got = lax.all_to_all(message, everyone, split_axis=0, concat_axis=0, tiled=True)

    def exchange(parts):
        moved = []
        for part, k in zip(parts, ORDER):
            if k:
                part = lax.ppermute(part, "gy", [(i, i ^ k) for i in range(N_GY)])
            moved.append(in_vmem(part))
        return moved

    station_coefs = exchange(
        pl.pallas_call(
            gather_kernel,
            out_shape=[pltpu.VMEM((LEV, DEV), F32)] * N_GY,
            in_specs=[vmem, vmem],
            out_specs=[vmem] * N_GY,
            scratch_shapes=[pltpu.VMEM((N_GY, LEV, DEV), F32)],
            name="gather",
        )(vertical_coef, in_vmem(codes)),
    )
    line = pltpu.VMEM((LEV, SLOTS), F32)
    station_lines = pl.pallas_call(
        station_coef_kernel,
        out_shape=[line] * 3,
        in_specs=[vmem] * N_GY,
        out_specs=[vmem] * 3,
        scratch_shapes=[pltpu.VMEM((N_GY, LEV, DEV), F32), pltpu.VMEM((LEV, SLOTS), F32)],
        name="station_coef",
    )(*station_coefs)
    product = smooth_call(in_vmem(got), inverse_x, inverse_y)
    parts = exchange(product)
    plane = pltpu.VMEM((LEV, CY, CX), F32)
    planes = call(coef_kernel, (plane, plane, plane), 1)(vertical_coef)
    picked = pl.pallas_call(
        station_kernel,
        out_shape=pltpu.VMEM((N_GX, N_GX, DEV), BF),
        in_specs=[vmem] * (N_GY + 3),
        out_specs=vmem,
        scratch_shapes=[
            pltpu.VMEM((LAYERS, SLOTS), F32),
            pltpu.VMEM((LAYERS, SLOTS), F32),
            pltpu.VMEM((SLOTS, DEV), F32),
        ],
        name="station",
    )(*parts, *[in_vmem(x) for x in station_lines])
    returned = lax.all_to_all(picked, "gx", split_axis=0, concat_axis=0, tiled=True)
    increment = pl.pallas_call(
        solve_kernel,
        out_shape=pltpu.VMEM((LAYERS, CY, CX), BF),
        in_specs=[vmem] * (N_GY + 4) + [pl.BlockSpec(memory_space=pl.ANY)],
        out_specs=vmem,
        scratch_shapes=[pltpu.VMEM((LAYERS, CY, CX), BF), pltpu.VMEM((LAYERS, CY, CX), F32)],
        name="solve",
    )(*parts, *[in_vmem(x) for x in planes], land_mask, picked)
    returned = returned.reshape(SLOTS, LAYERS).T.reshape(1, LAYERS, SLOTS)
    slot_index = lax.broadcasted_iota(I32, (DEV, CAP), 1)
    live = (slot_index < profile_counts[0][:, None]).reshape(SLOTS)
    equivalents = jnp.where(live[None, None, :], returned, jnp.zeros((), BF))
    return increment, equivalents


def solution(mesh):
    in_specs = (
        P(("gx", "gy"), None, None),
        P(("gx", "gy"), None),
        P(("gx", "gy"), None),
        P("gy", "gx"),
        P(None, "gy", "gx"),
        P(None, None, "gx"),
        P(),
    )
    out_specs = (P(None, "gy", "gx"), P(("gx", "gy"), None, None))
    return jax.shard_map(inner, mesh=mesh, in_specs=in_specs, out_specs=out_specs, check_vma=False)
```
